512 devices in a mesh: ctx: 64 (over z, y), tp: 8 (over x, core).
Axes of the slice: x: 4, y: 8, z: 8, core: 2. Of those that a mesh axis runs over, the one named last changes fastest.
Arguments:
- query_states: bfloat16 [32768, 4096], P('ctx', 'tp'), may hold values from -32 to 32
- rotated_key_states: bfloat16 [32768, 2048], P('ctx', 'tp'), may hold values from -32 to 32
- value_state_rows: bfloat16 [32768, 2048], P('ctx', 'tp'), may hold values from -6 to 6
- doc_ids: int32 [32768], P('ctx'), may hold values from 0 to 31, never falling along the last dimension, each value on 1 to 2048 neighbouring positions
- w_out: bfloat16 [4096, 5376], P('ctx', 'tp'), may hold values from -0.25 to 0.25
Outputs:
- mixed: bfloat16 [32768, 5376], P('ctx', 'tp')
The draws below stay inside these ranges and needn't reach their ends.
Inputs may be any that keep to these rules, and one draw needn't show every extreme that they name: `doc_ids`: document numbers never fall along the tokens; each document has 1 to 2048 tokens and one has exactly 2048.
All inputs are finite; a program needn't handle non-finite values.
Results may differ from the reference program's by a relative error of at most 0.0054.
Values may be sent and summed in bfloat16 or wider, within the bound.
No kernel may reach another device: no remote copies, remote signals or barrier semaphores. Data moves between devices by JAX's collectives and lax.ppermute only.
A program may use at most 64 MiB of HBM per device.

```python
import math
import jax
import jax.numpy as jnp
import numpy as np
from jax import lax

D = 5376
QUERY_HEAD_COUNT = 32
KEY_VALUE_HEADS = 16
HEAD_SIZE = 128
LOOKBACK_SPAN = 1024
PACKED_TOKENS = 32768
DOCS = 32
MOST = 2048


def draw_shared(key):
    random_key_split = jax.random.fold_in(key, 101)
    key_query = jax.random.fold_in(key, 102)
    key_matrix = jax.random.truncated_normal(random_key_split, -4.0, 4.0, (PACKED_TOKENS, KEY_VALUE_HEADS, HEAD_SIZE), jnp.float32)
    query_matrix = jax.random.truncated_normal(key_query, -4.0, 4.0, (PACKED_TOKENS, QUERY_HEAD_COUNT, HEAD_SIZE), jnp.float32)
    key_matrix = jnp.clip(key_matrix, -32.0, 32.0).reshape(PACKED_TOKENS, KEY_VALUE_HEADS * HEAD_SIZE)
    query_matrix = jnp.clip(query_matrix, -32.0, 32.0).reshape(PACKED_TOKENS, QUERY_HEAD_COUNT * HEAD_SIZE)
    return (query_matrix, key_matrix)


def draw_query_states(key, part):
    return draw_shared(key)[0].astype(jnp.bfloat16)


def draw_rotated_key_states(key, part):
    return draw_shared(key)[1].astype(jnp.bfloat16)


def strengthened(entries, own_key, source, target, shards_of, factor):
    def block_of(position):
        return (jnp.arange(entries.shape[position]) // (entries.shape[position] // shards_of)).reshape((-1,) + (1,) * (entries.ndim - 1 - position))

    first = jax.random.permutation(own_key, shards_of)[block_of(target)]
    far = (block_of(target) + shards_of // 2) % shards_of
    return jnp.where((block_of(source) == first) | (block_of(source) == far), factor * entries, entries)


def shard_levels(rng, extent, split, low, largest):
    def one(dim, shards_of):
        draws = jax.random.uniform(jax.random.fold_in(jax.random.fold_in(rng, 6), dim), (shards_of,), jnp.float32, low / len(split), largest / len(split))
        return jnp.repeat(jnp.exp(draws), extent[dim] // shards_of).reshape((-1,) + (1,) * (len(extent) - dim - 1))

    loudness = one(*split[0])
    for cut in split[1:]:
        loudness = loudness * one(*cut)
    return loudness


def length_profile(amount, total, bound, lean):
    loads = [(1 << 20) // math.isqrt(standing ** lean) + 1 for standing in range(2, amount + 1)]
    spare, counts = total - bound - (amount - 1), [1] * (amount - 1)
    while spare > 0:
        candidates = [i for i in range(amount - 1) if counts[i] < bound]
        mass, budget = sum([loads[i] for i in candidates]), spare
        for i in candidates:
            extra = min(bound - counts[i], max(1, budget * loads[i] // mass), spare)
            counts[i] = counts[i] + extra
            spare = spare - extra
    return np.array([bound] + counts)


def ragged_sizes(stream_key, amount, total, limit, lean):
    if amount == 2:
        one = jax.random.randint(stream_key, (), max(1, total - limit), min(limit, total - 1) + 1)
        return jnp.stack([one, total - one])
    sizes = jnp.asarray(length_profile(amount, total, limit, lean), jnp.int32)
    pairs = (amount - 1) // 2
    source_of, taker = sizes[1:1 + 2 * pairs:2], sizes[2:2 + 2 * pairs:2]
    margin = jnp.minimum(source_of - 1, limit - taker)
    shifted = jax.random.randint(jax.random.fold_in(stream_key, 1), (pairs,), 0, 1 << 20) % (margin + 1)
    sizes = sizes.at[1:1 + 2 * pairs:2].set(source_of - shifted).at[2:2 + 2 * pairs:2].set(taker + shifted)
    return sizes[jax.random.permutation(jax.random.fold_in(stream_key, 2), amount)]


def noise(own_key, dims, deviation, limit, pieces=(), kind=jnp.bfloat16):
    values = deviation * jax.random.normal(own_key, dims, jnp.float32)
    if pieces:
        values = values * shard_levels(own_key, dims, pieces, -0.22, 0.18)
    return jnp.clip(values, -limit, limit).astype(kind)


def noise_with(key, shape, deviation, reach, shards, heavy, held_as=jnp.bfloat16):
    entries = deviation * jax.random.normal(key, shape, jnp.float32)
    if shards:
        entries = entries * shard_levels(key, shape, shards, -0.22, 0.18)
    return jnp.clip(strengthened(entries, jax.random.fold_in(key, 3), *heavy), -reach, reach).astype(held_as)


def setup_inputs(seed: int = 0) -> dict:
    arg_keys = jax.random.split(jax.random.key(seed), 6)
    return {
        "query_states": draw_query_states(jax.random.fold_in(arg_keys[5], 71), 0),
        "rotated_key_states": draw_rotated_key_states(jax.random.fold_in(arg_keys[5], 71), 0),
        "value_state_rows": noise(arg_keys[2], (PACKED_TOKENS, KEY_VALUE_HEADS * HEAD_SIZE), 1.0, 6.0, ((0, 64), (1, 8))),
        "doc_ids": jnp.searchsorted(jnp.cumsum(ragged_sizes(arg_keys[3], DOCS, PACKED_TOKENS, MOST, 2)), jnp.arange(PACKED_TOKENS), side="right").astype(jnp.int32),
        "w_out": noise_with(arg_keys[4], (QUERY_HEAD_COUNT * HEAD_SIZE, D), (QUERY_HEAD_COUNT * HEAD_SIZE) ** -0.5, 0.25, ((0, 64), (1, 8)), (0, 1, 64, 4.0)),
    }


attn_scale = 168.0 ** -0.5


def attend(query_states, rotated_key_states, value_state_rows, doc_ids):
    queries_per_group = QUERY_HEAD_COUNT // KEY_VALUE_HEADS
    block_total = PACKED_TOKENS // LOOKBACK_SPAN
    padded_keys = jnp.concatenate([jnp.zeros((LOOKBACK_SPAN, KEY_VALUE_HEADS * HEAD_SIZE), rotated_key_states.dtype), rotated_key_states], 0)
    padded_values = jnp.concatenate([jnp.zeros((LOOKBACK_SPAN, KEY_VALUE_HEADS * HEAD_SIZE), value_state_rows.dtype), value_state_rows], 0)
    docs_pad = jnp.concatenate([jnp.full((LOOKBACK_SPAN,), -1, jnp.int32), doc_ids.astype(jnp.int32)], 0)

    def one_block(block_id):
        offset = (block_id * LOOKBACK_SPAN).astype(jnp.int32)
        query_row_block = lax.dynamic_slice_in_dim(query_states, offset, LOOKBACK_SPAN, 0).astype(jnp.float32)
        query_row_block = query_row_block.reshape(LOOKBACK_SPAN, KEY_VALUE_HEADS, queries_per_group, HEAD_SIZE)
        key_row_block = lax.dynamic_slice_in_dim(padded_keys, offset, 2 * LOOKBACK_SPAN, 0).astype(jnp.float32)
        key_row_block = key_row_block.reshape(2 * LOOKBACK_SPAN, KEY_VALUE_HEADS, HEAD_SIZE)
        value_row_block = lax.dynamic_slice_in_dim(padded_values, offset, 2 * LOOKBACK_SPAN, 0).astype(jnp.float32)
        value_row_block = value_row_block.reshape(2 * LOOKBACK_SPAN, KEY_VALUE_HEADS, HEAD_SIZE)
        query_docs = lax.dynamic_slice_in_dim(doc_ids.astype(jnp.int32), offset, LOOKBACK_SPAN, 0)
        key_docs = lax.dynamic_slice_in_dim(docs_pad, offset, 2 * LOOKBACK_SPAN, 0)
        query_pos = jnp.arange(LOOKBACK_SPAN, dtype=jnp.int32) + LOOKBACK_SPAN
        key_pos = jnp.arange(2 * LOOKBACK_SPAN, dtype=jnp.int32)
        distance = query_pos[:, None] - key_pos[None, :]
        visible = (query_docs[:, None] == key_docs[None, :]) & (distance >= 0) & (distance < LOOKBACK_SPAN)
        scores = jnp.einsum("qhgd,khd->hgqk", query_row_block, key_row_block) * attn_scale
        scores = jnp.where(visible, scores, -jnp.inf)
        row_max = jnp.max(scores, axis=3, keepdims=True)
        weights = jnp.exp(scores - row_max)
        weight_sum = jnp.sum(weights, axis=3)
        rounded = lax.optimization_barrier(weights.astype(jnp.bfloat16)).astype(jnp.float32)
        numer = jnp.einsum("hgqk,khd->qhgd", rounded, value_row_block)
        result = numer / jnp.transpose(weight_sum, (2, 0, 1))[..., None]
        return result.astype(jnp.bfloat16).reshape(LOOKBACK_SPAN, QUERY_HEAD_COUNT * HEAD_SIZE)

    blocks = lax.map(one_block, jnp.arange(block_total, dtype=jnp.int32))
    return blocks.reshape(PACKED_TOKENS, QUERY_HEAD_COUNT * HEAD_SIZE)


def reference(query_states, rotated_key_states, value_state_rows, doc_ids, w_out):
    attended = attend(query_states, rotated_key_states, value_state_rows, doc_ids)
    summed = jnp.dot(attended, w_out, preferred_element_type=jnp.float32)
    return summed.astype(jnp.bfloat16)
```

```python
import functools
import jax
import jax.numpy as jnp
from jax import lax
from jax.experimental import pallas as pl
from jax.experimental.pallas import tpu as pltpu
from jax.sharding import Mesh
from jax.sharding import PartitionSpec as P

HEAD_SIZE = 128
LOOKBACK_SPAN = 1024
NEG = -1e30
EXP_SCALE = 168.0 ** (-0.5) * 1.4426950408889634
TOK = 512
TILE = 256


def visible_tile(kind, k0, q0, rows, cols):
    key = lax.broadcasted_iota(jnp.int32, (rows, cols), 0) + k0
    query = lax.broadcasted_iota(jnp.int32, (rows, cols), 1) + q0
    if kind == 0:
        return key <= query
    if kind == 2:
        return key > query
    return None


def tile_needed(kind, k0, q0):
    if kind == 0:
        return k0 <= q0 + TILE - 1
    if kind == 2:
        return k0 + TILE - 1 > q0
    return True


def attend_kernel(kind, last, heads, *refs):
    if kind == 0:
        q_ref, k_ref, v_ref, row_ref, col_ref, acc_out, stat_out = refs
        kv_ref = None
    elif last:
        q_ref, kv_ref, row_ref, acc_ref, stat_ref, out_ref = refs
    else:
        q_ref, kv_ref, row_ref, acc_ref, stat_ref, acc_out, stat_out = refs
    kv_heads = heads // 2
    half = kv_heads * HEAD_SIZE
    q_docs = row_ref[...]
    for q0 in range(0, TOK, TILE):
        tiles = [k0 for k0 in range(0, TOK, TILE) if tile_needed(kind, k0, q0)]
        allowed = []
        for k0 in tiles:
            grid = visible_tile(kind, k0, q0, TILE, TILE)
            if kind == 0:
                keys = col_ref[k0 : k0 + TILE, :]
                same = jnp.concatenate(
                    [keys == q_docs[:, q0 + c : q0 + c + 128] for c in range(0, TILE, 128)], axis=1
                )
            else:
                first = q_docs[:, 0:1]
                k_docs = kv_ref[TOK : TOK + 1, :].astype(jnp.float32).astype(jnp.int32)
                before = jnp.sum(jnp.where(k_docs == first, 0, 1), axis=1, keepdims=True)
                key = lax.broadcasted_iota(jnp.int32, (TILE, TILE), 0) + k0
                same = (key >= before) & (q_docs[:, q0 : q0 + TILE] == first)
            allowed.append(same if grid is None else same & grid)
        for h in range(heads):
            g = h // 2
            q = q_ref[q0 : q0 + TILE, h * HEAD_SIZE : (h + 1) * HEAD_SIZE]
            scores = []
            for k0, ok in zip(tiles, allowed):
                if kind == 0:
                    k = k_ref[k0 : k0 + TILE, g * HEAD_SIZE : (g + 1) * HEAD_SIZE]
                else:
                    k = kv_ref[k0 : k0 + TILE, g * HEAD_SIZE : (g + 1) * HEAD_SIZE]
                s = lax.dot_general(k, q, (((1,), (1,)), ((), ())), preferred_element_type=jnp.float32)
                scores.append(jnp.where(ok, s, NEG))
            top = functools.reduce(jnp.maximum, [jnp.max(s, axis=0, keepdims=True) for s in scores])
            if kind != 0:
                old_top = stat_ref[h : h + 1, q0 : q0 + TILE]
                top = jnp.maximum(top, old_top)
                keep = jnp.exp2((old_top - top) * EXP_SCALE)
            weights = [jnp.exp2((s - top) * EXP_SCALE) for s in scores]
            total = functools.reduce(jnp.add, [jnp.sum(w, axis=0, keepdims=True) for w in weights])
            numer = None
            for k0, w in zip(tiles, weights):
                if kind == 0:
                    v = v_ref[k0 : k0 + TILE, g * HEAD_SIZE : (g + 1) * HEAD_SIZE]
                else:
                    v = kv_ref[k0 : k0 + TILE, half + g * HEAD_SIZE : half + (g + 1) * HEAD_SIZE]
                part = lax.dot_general(
                    v, w.astype(jnp.bfloat16), (((0,), (0,)), ((), ())), preferred_element_type=jnp.float32
                )
                numer = part if numer is None else numer + part
            rows = slice(h * HEAD_SIZE, (h + 1) * HEAD_SIZE)
            if kind != 0:
                total = total + stat_ref[heads + h : heads + h + 1, q0 : q0 + TILE] * keep
                numer = numer + acc_ref[rows, q0 : q0 + TILE] * keep
            if last:
                done = (numer / total).T
                out_ref[q0 : q0 + TILE, rows] = done.astype(jnp.bfloat16)
            else:
                acc_out[rows, q0 : q0 + TILE] = numer
                stat_out[h : h + 1, q0 : q0 + TILE] = top
                stat_out[heads + h : heads + h + 1, q0 : q0 + TILE] = total


VMEM = pl.BlockSpec(memory_space=pltpu.VMEM)


def attend(kind, last, heads, *args):
    width = heads * HEAD_SIZE
    if last:
        out = jax.ShapeDtypeStruct((TOK, width), jnp.bfloat16)
        specs = VMEM
    else:
        out = (
            jax.ShapeDtypeStruct((width, TOK), jnp.float32),
            jax.ShapeDtypeStruct((2 * heads, TOK), jnp.float32),
        )
        specs = (VMEM, VMEM)
    return pl.pallas_call(
        functools.partial(attend_kernel, kind, last, heads),
        out_shape=out,
        in_specs=[VMEM] * len(args),
        out_specs=specs,
        name="attend%d" % kind,
        cost_estimate=pl.CostEstimate(
            flops=4 * TOK * TOK * width, bytes_accessed=2 * 1024 * 1024, transcendentals=TOK * TOK * heads
        ),
    )(*args)


def project_kernel(chunks, at_ref, *refs):
    a_refs, w_ref, out_ref, full = refs[:-3], refs[-3], refs[-2], refs[-1]
    i = 0
    for slot, ref in enumerate(a_refs):
        column, row = chunks[slot]
        rows, cols = ref.shape
        lanes = pl.ds(pl.multiple_of(at_ref[column] * cols, cols), cols)
        full[row : row + rows, lanes] = ref[...]
    width = w_ref.shape[1]
    for n0 in range(0, width, 256):
        n1 = min(n0 + 256, width)
        got = jnp.dot(full[...], w_ref[:, n0:n1], preferred_element_type=jnp.float32)
        out_ref[n0:n1, :] = got.T.astype(jnp.bfloat16)


def project(chunks, at, arrays, w):
    width = w.shape[1]
    return pl.pallas_call(
        functools.partial(project_kernel, chunks),
        out_shape=jax.ShapeDtypeStruct((width, TOK), jnp.bfloat16),
        in_specs=[pl.BlockSpec(memory_space=pltpu.SMEM)] + [VMEM] * (len(arrays) + 1),
        out_specs=VMEM,
        scratch_shapes=[pltpu.VMEM((TOK, w.shape[0]), jnp.bfloat16)],
        name="project",
        cost_estimate=pl.CostEstimate(
            flops=2 * TOK * w.shape[0] * width, bytes_accessed=12 * 1024 * 1024, transcendentals=0
        ),
    )(at, *arrays, w)


def body(query_states, rotated_key_states, value_state_rows, doc_ids, w_out):
    heads = query_states.shape[1] // HEAD_SIZE
    zs, ys, xs = lax.axis_size("z"), lax.axis_size("y"), lax.axis_size("x")
    blocks = zs * ys
    onward = [(i, i + 1) for i in range(blocks - 1)]
    block = lax.axis_index("z") * ys + lax.axis_index("y")
    w_all = lax.all_gather(w_out, ("z", "y"), axis=0, tiled=True)

    docs_row = jnp.broadcast_to(doc_ids.astype(jnp.bfloat16)[None, :], (16, TOK))
    packed = jnp.concatenate(
        [jnp.concatenate([rotated_key_states, value_state_rows], axis=1), docs_row], axis=0
    )
    one_back = lax.ppermute(packed, ("z", "y"), onward)
    two_back = lax.ppermute(one_back, ("z", "y"), onward)

    row = doc_ids[None, :]
    col = jnp.broadcast_to(doc_ids[:, None], (TOK, 128))
    row_one = jnp.where(block >= 1, row, -1 - row)
    row_two = jnp.where(block >= 2, row, -1 - row)
    acc, stat = attend(0, False, heads, query_states, rotated_key_states, value_state_rows, row, col)
    acc, stat = attend(1, False, heads, query_states, one_back, row_one, acc, stat)
    mine = attend(2, True, heads, query_states, two_back, row_two, acc, stat)

    def along(value, axis, by):
        n = lax.axis_size(axis)
        return lax.ppermute(value, axis, [(i, (i + by) % n) for i in range(n)])

    half = TOK // 2
    low = along(mine, "x", 1)
    high = along(mine, "x", -1)
    far_top = along(low[:half], "x", 1)
    far_bottom = along(high[half:], "x", -1)
    mate = [along(v, "core", 1) for v in (mine, low, high, far_top, far_bottom)]
    x, core = lax.axis_index("x"), lax.axis_index("core")
    spots = [x, (x + xs - 1) % xs, (x + 1) % xs, (x + 2) % xs]
    at = jnp.stack([s * 2 + core for s in spots] + [s * 2 + 1 - core for s in spots]).astype(jnp.int32)
    where = [(0, 0), (1, 0), (2, 0), (3, 0), (3, half)]
    chunks = where + [(c + 4, r) for c, r in where]
    out = project(chunks, at, [mine, low, high, far_top, far_bottom] + mate, w_all)
    return out.T


def solution(mesh):
    zs, ys = 8, 8
    fine = Mesh(mesh.devices.reshape(zs, ys, 4, 2), ("z", "y", "x", "core"))
    ctx, tp = ("z", "y"), ("x", "core")
    return jax.shard_map(
        body,
        mesh=fine,
        in_specs=(P(ctx, tp), P(ctx, tp), P(ctx, tp), P(ctx), P(ctx, tp)),
        out_specs=P(ctx, tp),
        check_vma=False,
    )
```

```python
import functools
import jax
import jax.numpy as jnp
from jax import lax
from jax.experimental import pallas as pl
from jax.experimental.pallas import tpu as pltpu
from jax.sharding import Mesh
from jax.sharding import PartitionSpec as P


HEAD_SIZE = 128
NEG = -1e30
EXP_SCALE = 168.0 ** (-0.5) * 1.4426950408889634
TOK = 512
TILE = 256


def visible_tile(kind, k0, q0, rows, cols):
    key = lax.broadcasted_iota(jnp.int32, (rows, cols), 0) + k0
    query = lax.broadcasted_iota(jnp.int32, (rows, cols), 1) + q0
    if kind == 0:
        return key <= query
    if kind == 2:
        return key > query
    return None


def tile_needed(kind, k0, q0):
    if kind == 0:
        return k0 <= q0 + TILE - 1
    if kind == 2:
        return k0 + TILE - 1 > q0
    return True


def attend_kernel(kind, last, heads, *refs):
    if kind == 0:
        q_ref, k_ref, v_ref, row_ref, col_ref, acc_out, stat_out = refs
        kv_ref = None
    elif last:
        core_ref, q_ref, kv_ref, row_ref, acc_ref, stat_ref, keep_ref, send_ref = refs
        first_core = core_ref[0] == 0
    else:
        q_ref, kv_ref, row_ref, acc_ref, stat_ref, acc_out, stat_out = refs
    kv_heads = heads // 2
    half = kv_heads * HEAD_SIZE
    q_docs = row_ref[...]
    for q0 in range(0, TOK, TILE):
        tiles = [k0 for k0 in range(0, TOK, TILE) if tile_needed(kind, k0, q0)]
        allowed = []
        for k0 in tiles:
            grid = visible_tile(kind, k0, q0, TILE, TILE)
            if kind == 0:
                keys = col_ref[k0 : k0 + TILE, :]
                same = jnp.concatenate(
                    [keys == q_docs[:, q0 + c : q0 + c + 128] for c in range(0, TILE, 128)], axis=1
                )
            else:
                first = q_docs[:, 0:1]
                k_docs = kv_ref[TOK : TOK + 1, :].astype(jnp.float32).astype(jnp.int32)
                before = jnp.sum(jnp.where(k_docs == first, 0, 1), axis=1, keepdims=True)
                key = lax.broadcasted_iota(jnp.int32, (TILE, TILE), 0) + k0
                same = (key >= before) & (q_docs[:, q0 : q0 + TILE] == first)
            allowed.append(same if grid is None else same & grid)
        kept, sent = [], []
        for h in range(heads):
            g = h // 2
            q = q_ref[q0 : q0 + TILE, h * HEAD_SIZE : (h + 1) * HEAD_SIZE]
            scores = []
            for k0, ok in zip(tiles, allowed):
                if kind == 0:
                    k = k_ref[k0 : k0 + TILE, g * HEAD_SIZE : (g + 1) * HEAD_SIZE]
                else:
                    k = kv_ref[k0 : k0 + TILE, g * HEAD_SIZE : (g + 1) * HEAD_SIZE]
                s = lax.dot_general(k, q, (((1,), (1,)), ((), ())), preferred_element_type=jnp.float32)
                scores.append(jnp.where(ok, s, NEG))
            top = functools.reduce(jnp.maximum, [jnp.max(s, axis=0, keepdims=True) for s in scores])
            if kind != 0:
                old_top = stat_ref[h : h + 1, q0 : q0 + TILE]
                top = jnp.maximum(top, old_top)
                keep = jnp.exp2((old_top - top) * EXP_SCALE)
            weights = [jnp.exp2((s - top) * EXP_SCALE) for s in scores]
            total = functools.reduce(jnp.add, [jnp.sum(w, axis=0, keepdims=True) for w in weights])
            numer = None
            for k0, w in zip(tiles, weights):
                if kind == 0:
                    v = v_ref[k0 : k0 + TILE, g * HEAD_SIZE : (g + 1) * HEAD_SIZE]
                else:
                    v = kv_ref[k0 : k0 + TILE, half + g * HEAD_SIZE : half + (g + 1) * HEAD_SIZE]
                part = lax.dot_general(
                    v, w.astype(jnp.bfloat16), (((0,), (0,)), ((), ())), preferred_element_type=jnp.float32
                )
                numer = part if numer is None else numer + part
            rows = slice(h * HEAD_SIZE, (h + 1) * HEAD_SIZE)
            if kind != 0:
                total = total + stat_ref[heads + h : heads + h + 1, q0 : q0 + TILE] * keep
                numer = numer + acc_ref[rows, q0 : q0 + TILE] * keep
            if last:
                done = numer / total
                low_rows = jnp.concatenate([done[0:32], done[64:96]], axis=0)
                high_rows = jnp.concatenate([done[32:64], done[96:128]], axis=0)
                kept.append(jnp.where(first_core, low_rows, high_rows))
                sent.append(jnp.where(first_core, high_rows, low_rows))
            else:
                acc_out[rows, q0 : q0 + TILE] = numer
                stat_out[h : h + 1, q0 : q0 + TILE] = top
                stat_out[heads + h : heads + h + 1, q0 : q0 + TILE] = total
        if last:
            for ref, pieces in ((keep_ref, kept), (send_ref, sent)):
                for p in range(0, heads, 2):
                    both = jnp.concatenate(pieces[p : p + 2], axis=0).T
                    ref[q0 : q0 + TILE, p * 64 : p * 64 + 128] = both.astype(jnp.bfloat16)


VMEM = pl.BlockSpec(memory_space=pltpu.VMEM)
SMEM = pl.BlockSpec(memory_space=pltpu.SMEM)


def attend(kind, last, heads, *args):
    width = heads * HEAD_SIZE
    if last:
        out = (jax.ShapeDtypeStruct((TOK, width // 2), jnp.bfloat16),) * 2
    else:
        out = (
            jax.ShapeDtypeStruct((width, TOK), jnp.float32),
            jax.ShapeDtypeStruct((2 * heads, TOK), jnp.float32),
        )
    return pl.pallas_call(
        functools.partial(attend_kernel, kind, last, heads),
        out_shape=out,
        in_specs=([SMEM] if last else []) + [VMEM] * (len(args) - (1 if last else 0)),
        out_specs=(VMEM, VMEM),
        compiler_params=pltpu.CompilerParams(vmem_limit_bytes=16 << 20),
        cost_estimate=pl.CostEstimate(
            flops=4 * TOK * TOK * width, bytes_accessed=2 * 1024 * 1024, transcendentals=TOK * TOK * heads
        ),
    )(*args)


def project_kernel(spots, counts, cut, at_ref, pos_ref, *refs):
    n_a, n_w = len(spots), len(counts)
    a_refs, w_refs = refs[:n_a], refs[n_a : n_a + n_w]
    own_ref, other_ref, a_full, w_full = refs[n_a + n_w :]
    for (slot, shift, row), ref in zip(spots, a_refs):
        rows, cols = ref.shape
        lanes = pl.ds(pl.multiple_of(at_ref[slot] * 512 + shift, 256), cols)
        a_full[row : row + rows, lanes] = ref[...]
    k = 0
    for count, ref in zip(counts, w_refs):
        for i in range(count):
            place = pl.ds(pl.multiple_of(pos_ref[k] * 32, 32), 32)
            w_full[place, :] = ref[i * 32 : i * 32 + 32, :]
            k += 1
    main, own, width = cut
    other = width - own
    for n0 in range(0, width, 256):
        n1 = min(n0 + 256, width)
        got = jnp.dot(a_full[...], w_full[:, n0:n1], preferred_element_type=jnp.float32).T
        for lo, hi, ref, base in (
            (0, main, own_ref, 0),
            (main, main + other, other_ref, 0),
            (main + other, width, own_ref, main),
        ):
            s0, s1 = max(lo, n0), min(hi, n1)
            if s0 < s1:
                ref[base + s0 - lo : base + s1 - lo, :] = got[s0 - n0 : s1 - n0].astype(ref.dtype)


def project(spots, counts, cut, at, pos, a_arrays, w_arrays):
    depth = sum(counts) * 32
    own, width = cut[1:]
    return pl.pallas_call(
        functools.partial(project_kernel, spots, counts, cut),
        out_shape=(
            jax.ShapeDtypeStruct((own, TOK), jnp.float32),
            jax.ShapeDtypeStruct((width - own, TOK), jnp.bfloat16),
        ),
        in_specs=[SMEM, SMEM] + [VMEM] * (len(a_arrays) + len(w_arrays)),
        out_specs=(VMEM, VMEM),
        scratch_shapes=[pltpu.VMEM((TOK, depth), jnp.bfloat16), pltpu.VMEM((depth, w_arrays[0].shape[1]), jnp.bfloat16)],
        name="project",
        compiler_params=pltpu.CompilerParams(vmem_limit_bytes=36 << 20),
        cost_estimate=pl.CostEstimate(
            flops=2 * TOK * depth * width, bytes_accessed=12 * 1024 * 1024, transcendentals=0
        ),
    )(at, pos, *a_arrays, *w_arrays)


def along(value, axis, by):
    n = lax.axis_size(axis)
    return lax.ppermute(value, axis, [(i, (i + by) % n) for i in range(n)])


def moved(z, y, by, along_z):
    return ((z + by) % 8, y) if along_z else (z, (y + by) % 8)


def spot(z, y, core):
    return (z * 8 + y) * 2 + core


def spread(value):
    groups = []
    for core in range(2):
        for k in range(8):
            groups.append([spot(i, k, core) if core == 0 else spot(k, i, core) for i in range(8)])
    copies = jnp.broadcast_to(value[None], (8,) + value.shape)
    got = lax.all_to_all(copies, ("z", "y", "core"), 0, 0, axis_index_groups=groups)
    return got.reshape(8 * value.shape[0], value.shape[1])


def ring(value, by):
    pairs = []
    for z in range(8):
        for y in range(8):
            for core in range(2):
                pairs.append((spot(z, y, core), spot(*moved(z, y, by, core == 1), core)))
    return lax.ppermute(value, ("z", "y", "core"), pairs)


def layer(query_states, rotated_key_states, value_state_rows, doc_ids, w_out):
    heads = query_states.shape[1] // HEAD_SIZE
    zs, ys, xs = lax.axis_size("z"), lax.axis_size("y"), lax.axis_size("x")
    z, y, x, core = (lax.axis_index(n) for n in ("z", "y", "x", "core"))
    blocks = zs * ys
    onward = [(i, i + 1) for i in range(blocks - 1)]
    block = z * ys + y

    docs_row = jnp.broadcast_to(doc_ids.astype(jnp.bfloat16)[None, :], (16, TOK))
    packed = jnp.concatenate(
        [jnp.concatenate([rotated_key_states, value_state_rows], axis=1), docs_row], axis=0
    )
    one_back = lax.ppermute(packed, ("z", "y"), onward)
    two_back = lax.ppermute(one_back, ("z", "y"), onward)

    part, cols = w_out.shape[0] // 2, w_out.shape[1]
    main = cols // 128 * 128
    keep_w = jnp.where(core == 0, w_out[:part], w_out[part:])
    send_w = jnp.where(core == 0, w_out[part:], w_out[:part])
    got_w = along(send_w, "core", 1)
    fill = -2 * cols % 128
    seed = jnp.concatenate(
        [keep_w[:, :main], got_w, keep_w[:, main:], jnp.zeros((part, fill), w_out.dtype)], axis=1
    )
    own_cut = (main, cols, 2 * cols)

    whole = [spread(seed)]
    up = down = whole[0]
    offsets = [0]
    for step in range(1, 4):
        up, down = ring(up, 1), ring(down, -1)
        whole += [up, down]
        offsets += [-step, step]
    whole.append(ring(down, -1))
    offsets.append(4)
    spread_at = jnp.tile(jnp.arange(8, dtype=jnp.int32), 8)
    ring_at = jnp.repeat(jnp.array(offsets, jnp.int32), 8) + jnp.where(core == 0, y, z)
    wz = jnp.where(core == 0, spread_at, ring_at & 7)
    wy = jnp.where(core == 0, ring_at & 7, spread_at)
    pos = ((wz >> 1) * 2 + ((wz & 1) ^ core)) * 8 + wy

    row = doc_ids[None, :]
    col = jnp.broadcast_to(doc_ids[:, None], (TOK, 128))
    row_one = jnp.where(block >= 1, row, -1 - row)
    row_two = jnp.where(block >= 2, row, -1 - row)
    acc, stat = attend(0, False, heads, query_states, rotated_key_states, value_state_rows, row, col)
    acc, stat = attend(1, False, heads, query_states, one_back, row_one, acc, stat)
    core_word = jnp.full((1,), core, jnp.int32)
    keep, send = attend(2, True, heads, core_word, query_states, two_back, row_two, acc, stat)
    mate = along(send, "core", 1)
    pair = jnp.concatenate([keep, mate], axis=1)

    half = TOK // 2
    low = along(pair, "x", 1)
    high = along(pair, "x", -1)
    far_top = along(low[:half], "x", 1)
    far_bottom = along(high[half:], "x", -1)
    at = jnp.stack([x, (x + xs - 1) % xs, (x + 1) % xs, (x + 2) % xs]).astype(jnp.int32)
    spots = [(0, 0, 0), (1, 0, 0), (2, 0, 0), (3, 0, 0), (3, 0, half)]
    counts = (8,) * 8
    own, other = project(
        spots, counts, own_cut, at, pos.astype(jnp.int32), [pair, low, high, far_top, far_bottom], whole
    )
    back = along(other, "core", 1)
    return (own + back.astype(jnp.float32)).astype(jnp.bfloat16).T


def solution(mesh):
    zs, ys = 8, 8
    fine = Mesh(mesh.devices.reshape(zs, ys, 4, 2), ("z", "y", "x", "core"))
    ctx, tp = ("z", "y"), ("x", "core")
    return jax.shard_map(
        layer,
        mesh=fine,
        in_specs=(P(ctx, tp), P(ctx, tp), P(ctx, tp), P(ctx), P(ctx, tp)),
        out_specs=P(ctx, tp),
        check_vma=False,
    )
```

```python
import functools
import jax
import jax.numpy as jnp
from jax import lax
from jax.experimental import pallas as pl
from jax.experimental.pallas import tpu as pltpu
from jax.sharding import Mesh
from jax.sharding import PartitionSpec as P


HEAD_SIZE = 128
NEG = -1e30
EXP_SCALE = 168.0 ** (-0.5) * 1.4426950408889634
TOK = 512
TILE = 256


def visible_tile(kind, k0, q0, rows, cols):
    key = lax.broadcasted_iota(jnp.int32, (rows, cols), 0) + k0
    query = lax.broadcasted_iota(jnp.int32, (rows, cols), 1) + q0
    if kind == 0:
        return key <= query
    if kind == 2:
        return key > query
    return None


def tile_needed(kind, k0, q0):
    if kind == 0:
        return k0 <= q0 + TILE - 1
    if kind == 2:
        return k0 + TILE - 1 > q0
    return True


def attend_kernel(kind, last, heads, *refs):
    if kind == 0:
        q_ref, k_ref, v_ref, row_ref, col_ref, acc_out, stat_out = refs
        kv_ref = None
    elif last:
        q_ref, kv_ref, row_ref, acc_ref, stat_ref, out_ref = refs
    else:
        q_ref, kv_ref, row_ref, acc_ref, stat_ref, acc_out, stat_out = refs
    kv_heads = heads // 2
    half = kv_heads * HEAD_SIZE
    q_docs = row_ref[...]
    for q0 in range(0, TOK, TILE):
        tiles = [k0 for k0 in range(0, TOK, TILE) if tile_needed(kind, k0, q0)]
        allowed = []
        for k0 in tiles:
            grid = visible_tile(kind, k0, q0, TILE, TILE)
            if kind == 0:
                keys = col_ref[k0 : k0 + TILE, :]
                same = jnp.concatenate(
                    [keys == q_docs[:, q0 + c : q0 + c + 128] for c in range(0, TILE, 128)], axis=1
                )
            else:
                first = q_docs[:, 0:1]
                k_docs = kv_ref[TOK : TOK + 1, :].astype(jnp.float32).astype(jnp.int32)
                before = jnp.sum(jnp.where(k_docs == first, 0, 1), axis=1, keepdims=True)
                key = lax.broadcasted_iota(jnp.int32, (TILE, TILE), 0) + k0
                same = (key >= before) & (q_docs[:, q0 : q0 + TILE] == first)
            allowed.append(same if grid is None else same & grid)
        halves = ([], [])
        for h in range(heads):
            g = h // 2
            q = q_ref[q0 : q0 + TILE, h * HEAD_SIZE : (h + 1) * HEAD_SIZE]
            scores = []
            for k0, ok in zip(tiles, allowed):
                if kind == 0:
                    k = k_ref[k0 : k0 + TILE, g * HEAD_SIZE : (g + 1) * HEAD_SIZE]
                else:
                    k = kv_ref[k0 : k0 + TILE, g * HEAD_SIZE : (g + 1) * HEAD_SIZE]
                s = lax.dot_general(k, q, (((1,), (1,)), ((), ())), preferred_element_type=jnp.float32)
                scores.append(jnp.where(ok, s, NEG))
            top = functools.reduce(jnp.maximum, [jnp.max(s, axis=0, keepdims=True) for s in scores])
            if kind != 0:
                old_top = stat_ref[h : h + 1, q0 : q0 + TILE]
                top = jnp.maximum(top, old_top)
                keep = jnp.exp2((old_top - top) * EXP_SCALE)
            weights = [jnp.exp2((s - top) * EXP_SCALE) for s in scores]
            total = functools.reduce(jnp.add, [jnp.sum(w, axis=0, keepdims=True) for w in weights])
            numer = None
            for k0, w in zip(tiles, weights):
                if kind == 0:
                    v = v_ref[k0 : k0 + TILE, g * HEAD_SIZE : (g + 1) * HEAD_SIZE]
                else:
                    v = kv_ref[k0 : k0 + TILE, half + g * HEAD_SIZE : half + (g + 1) * HEAD_SIZE]
                part = lax.dot_general(
                    v, w.astype(jnp.bfloat16), (((0,), (0,)), ((), ())), preferred_element_type=jnp.float32
                )
                numer = part if numer is None else numer + part
            rows = slice(h * HEAD_SIZE, (h + 1) * HEAD_SIZE)
            if kind != 0:
                total = total + stat_ref[heads + h : heads + h + 1, q0 : q0 + TILE] * keep
                numer = numer + acc_ref[rows, q0 : q0 + TILE] * keep
            if last:
                done = numer / total
                halves[0].append(jnp.concatenate([done[0:32], done[64:96]], axis=0))
                halves[1].append(jnp.concatenate([done[32:64], done[96:128]], axis=0))
            else:
                acc_out[rows, q0 : q0 + TILE] = numer
                stat_out[h : h + 1, q0 : q0 + TILE] = top
                stat_out[heads + h : heads + h + 1, q0 : q0 + TILE] = total
        if last:
            for core in range(2):
                for p in range(0, heads, 2):
                    both = jnp.concatenate(halves[core][p : p + 2], axis=0).T.astype(jnp.bfloat16)
                    for to in range(core, out_ref.shape[0], 2):
                        out_ref[to, q0 : q0 + TILE, p * 64 : p * 64 + 128] = both


VMEM = pl.BlockSpec(memory_space=pltpu.VMEM)
SMEM = pl.BlockSpec(memory_space=pltpu.SMEM)


def attend(kind, last, heads, *args):
    width = heads * HEAD_SIZE
    if last:
        out = jax.ShapeDtypeStruct((8, TOK, width // 2), jnp.bfloat16)
    else:
        out = (
            jax.ShapeDtypeStruct((width, TOK), jnp.float32),
            jax.ShapeDtypeStruct((2 * heads, TOK), jnp.float32),
        )
    return pl.pallas_call(
        functools.partial(attend_kernel, kind, last, heads),
        out_shape=out,
        in_specs=[VMEM] * len(args),
        out_specs=VMEM if last else (VMEM, VMEM),
        compiler_params=pltpu.CompilerParams(vmem_limit_bytes=16 << 20),
        cost_estimate=pl.CostEstimate(
            flops=4 * TOK * TOK * width, bytes_accessed=2 * 1024 * 1024, transcendentals=TOK * TOK * heads
        ),
    )(*args)


def project_kernel(counts, cut, pos_ref, a_ref, *refs):
    w_refs, (own_ref, other_ref, a_full, w_full) = refs[:-4], refs[-4:]
    share = a_ref.shape[2]
    for t in range(a_ref.shape[0]):
        a_full[:, t * share : (t + 1) * share] = a_ref[t]
    k = 0
    for count, ref in zip(counts, w_refs):
        for i in range(count):
            place = pl.ds(pl.multiple_of(pos_ref[k] * 32, 32), 32)
            w_full[place, :] = ref[i * 32 : i * 32 + 32, :]
            k += 1
    main, own, width = cut
    other = width - own
    for n0 in range(0, width, 256):
        n1 = min(n0 + 256, width)
        got = jnp.dot(a_full[...], w_full[:, n0:n1], preferred_element_type=jnp.float32).T
        for lo, hi, ref, base in (
            (0, main, own_ref, 0),
            (main, main + other, other_ref, 0),
            (main + other, width, own_ref, main),
        ):
            s0, s1 = max(lo, n0), min(hi, n1)
            if s0 < s1:
                ref[base + s0 - lo : base + s1 - lo, :] = got[s0 - n0 : s1 - n0].astype(ref.dtype)


def project(counts, cut, pos, dealt, w_arrays):
    depth = sum(counts) * 32
    own, width = cut[1:]
    return pl.pallas_call(
        functools.partial(project_kernel, counts, cut),
        out_shape=(
            jax.ShapeDtypeStruct((own, TOK), jnp.float32),
            jax.ShapeDtypeStruct((width - own, TOK), jnp.bfloat16),
        ),
        in_specs=[SMEM] + [VMEM] * (1 + len(w_arrays)),
        out_specs=(VMEM, VMEM),
        scratch_shapes=[pltpu.VMEM((TOK, depth), jnp.bfloat16), pltpu.VMEM((depth, w_arrays[0].shape[1]), jnp.bfloat16)],
        name="project",
        compiler_params=pltpu.CompilerParams(vmem_limit_bytes=36 << 20),
        cost_estimate=pl.CostEstimate(
            flops=2 * TOK * depth * width, bytes_accessed=12 * 1024 * 1024, transcendentals=0
        ),
    )(pos, dealt, *w_arrays)


def along(value, axis, by):
    n = lax.axis_size(axis)
    return lax.ppermute(value, axis, [(i, (i + by) % n) for i in range(n)])


def moved(z, y, by, along_z):
    return ((z + by) % 8, y) if along_z else (z, (y + by) % 8)


def spot(z, y, core):
    return (z * 8 + y) * 2 + core


def spread(value):
    groups = []
    for core in range(2):
        for k in range(8):
            groups.append([spot(i, k, core) if core == 0 else spot(k, i, core) for i in range(8)])
    copies = jnp.broadcast_to(value[None], (8,) + value.shape)
    got = lax.all_to_all(copies, ("z", "y", "core"), 0, 0, axis_index_groups=groups)
    return got.reshape(8 * value.shape[0], value.shape[1])


def ring(value, by):
    pairs = []
    for z in range(8):
        for y in range(8):
            for core in range(2):
                pairs.append((spot(z, y, core), spot(*moved(z, y, by, core == 1), core)))
    return lax.ppermute(value, ("z", "y", "core"), pairs)


def layer(query_states, rotated_key_states, value_state_rows, doc_ids, w_out):
    heads = query_states.shape[1] // HEAD_SIZE
    zs, ys = lax.axis_size("z"), lax.axis_size("y")
    z, y, core = (lax.axis_index(n) for n in ("z", "y", "core"))
    blocks = zs * ys
    onward = [(i, i + 1) for i in range(blocks - 1)]
    block = z * ys + y

    docs_row = jnp.broadcast_to(doc_ids.astype(jnp.bfloat16)[None, :], (16, TOK))
    packed = jnp.concatenate(
        [jnp.concatenate([rotated_key_states, value_state_rows], axis=1), docs_row], axis=0
    )
    one_back = lax.ppermute(packed, ("z", "y"), onward)
    two_back = lax.ppermute(one_back, ("z", "y"), onward)

    part, cols = w_out.shape[0] // 2, w_out.shape[1]
    main = cols // 128 * 128
    keep_w = jnp.where(core == 0, w_out[:part], w_out[part:])
    send_w = jnp.where(core == 0, w_out[part:], w_out[:part])
    got_w = along(send_w, "core", 1)
    fill = -2 * cols % 128
    seed = jnp.concatenate(
        [keep_w[:, :main], got_w, keep_w[:, main:], jnp.zeros((part, fill), w_out.dtype)], axis=1
    )
    own_cut = (main, cols, 2 * cols)

    whole = [spread(seed)]
    up = down = whole[0]
    offsets = [0]
    for step in range(1, 4):
        up, down = ring(up, 1), ring(down, -1)
        whole += [up, down]
        offsets += [-step, step]
    whole.append(ring(down, -1))
    offsets.append(4)
    spread_at = jnp.tile(jnp.arange(8, dtype=jnp.int32), 8)
    ring_at = jnp.repeat(jnp.array(offsets, jnp.int32), 8) + jnp.where(core == 0, y, z)
    wz = jnp.where(core == 0, spread_at, ring_at & 7)
    wy = jnp.where(core == 0, ring_at & 7, spread_at)
    pos = wz * 8 + wy

    row = doc_ids[None, :]
    col = jnp.broadcast_to(doc_ids[:, None], (TOK, 128))
    row_one = jnp.where(block >= 1, row, -1 - row)
    row_two = jnp.where(block >= 2, row, -1 - row)
    acc, stat = attend(0, False, heads, query_states, rotated_key_states, value_state_rows, row, col)
    acc, stat = attend(1, False, heads, query_states, one_back, row_one, acc, stat)
    mine = attend(2, True, heads, query_states, two_back, row_two, acc, stat)
    dealt = lax.all_to_all(mine, ("x", "core"), 0, 0)
    own, other = project((8,) * 8, own_cut, pos.astype(jnp.int32), dealt, whole)
    back = along(other, "core", 1)
    return (own + back.astype(jnp.float32)).astype(jnp.bfloat16).T


def solution(mesh):
    zs, ys = 8, 8
    fine = Mesh(mesh.devices.reshape(zs, ys, 4, 2), ("z", "y", "x", "core"))
    ctx, tp = ("z", "y"), ("x", "core")
    return jax.shard_map(
        layer,
        mesh=fine,
        in_specs=(P(ctx, tp), P(ctx, tp), P(ctx, tp), P(ctx), P(ctx, tp)),
        out_specs=P(ctx, tp),
        check_vma=False,
    )
```

```python
import functools
import jax
import jax.numpy as jnp
from jax import lax
from jax.experimental import pallas as pl
from jax.experimental.pallas import tpu as pltpu
from jax.sharding import Mesh
from jax.sharding import PartitionSpec as P


HEAD_SIZE = 128
NEG = -1e30
EXP_SCALE = 168.0 ** (-0.5) * 1.4426950408889634
TOK = 512
TILE = 256


def visible_tile(kind, k0, q0, rows, cols):
    key = lax.broadcasted_iota(jnp.int32, (rows, cols), 0) + k0
    query = lax.broadcasted_iota(jnp.int32, (rows, cols), 1) + q0
    if kind == 0:
        return key <= query
    if kind == 2:
        return key > query
    return None


def tile_needed(kind, k0, q0):
    if kind == 0:
        return k0 <= q0 + TILE - 1
    if kind == 2:
        return k0 + TILE - 1 > q0
    return True


def attend_kernel(kind, last, heads, *refs):
    if kind == 0:
        q_ref, k_ref, v_ref, row_ref, col_ref, acc_out, stat_out = refs
        kv_ref = None
    elif last:
        q_ref, kv_ref, row_ref, acc_ref, stat_ref, out_ref = refs
    else:
        q_ref, kv_ref, row_ref, acc_ref, stat_ref, acc_out, stat_out = refs
    kv_heads = heads // 2
    half = kv_heads * HEAD_SIZE
    q_docs = row_ref[...]
    for q0 in range(0, TOK, TILE):
        tiles = [k0 for k0 in range(0, TOK, TILE) if tile_needed(kind, k0, q0)]
        allowed = []
        for k0 in tiles:
            grid = visible_tile(kind, k0, q0, TILE, TILE)
            if kind == 0:
                keys = col_ref[k0 : k0 + TILE, :]
                same = jnp.concatenate(
                    [keys == q_docs[:, q0 + c : q0 + c + 128] for c in range(0, TILE, 128)], axis=1
                )
            else:
                first = q_docs[:, 0:1]
                k_docs = kv_ref[TOK : TOK + 1, :].astype(jnp.float32).astype(jnp.int32)
                before = jnp.sum(jnp.where(k_docs == first, 0, 1), axis=1, keepdims=True)
                key = lax.broadcasted_iota(jnp.int32, (TILE, TILE), 0) + k0
                same = (key >= before) & (q_docs[:, q0 : q0 + TILE] == first)
            allowed.append(same if grid is None else same & grid)
        halves = ([], [])
        for h in range(heads):
            g = h // 2
            q = q_ref[q0 : q0 + TILE, h * HEAD_SIZE : (h + 1) * HEAD_SIZE]
            scores = []
            for k0, ok in zip(tiles, allowed):
                if kind == 0:
                    k = k_ref[k0 : k0 + TILE, g * HEAD_SIZE : (g + 1) * HEAD_SIZE]
                else:
                    k = kv_ref[k0 : k0 + TILE, g * HEAD_SIZE : (g + 1) * HEAD_SIZE]
                s = lax.dot_general(k, q, (((1,), (1,)), ((), ())), preferred_element_type=jnp.float32)
                scores.append(jnp.where(ok, s, NEG))
            top = functools.reduce(jnp.maximum, [jnp.max(s, axis=0, keepdims=True) for s in scores])
            if kind != 0:
                old_top = stat_ref[h : h + 1, q0 : q0 + TILE]
                top = jnp.maximum(top, old_top)
                keep = jnp.exp2((old_top - top) * EXP_SCALE)
            weights = [jnp.exp2((s - top) * EXP_SCALE) for s in scores]
            total = functools.reduce(jnp.add, [jnp.sum(w, axis=0, keepdims=True) for w in weights])
            numer = None
            for k0, w in zip(tiles, weights):
                if kind == 0:
                    v = v_ref[k0 : k0 + TILE, g * HEAD_SIZE : (g + 1) * HEAD_SIZE]
                else:
                    v = kv_ref[k0 : k0 + TILE, half + g * HEAD_SIZE : half + (g + 1) * HEAD_SIZE]
                part = lax.dot_general(
                    v, w.astype(jnp.bfloat16), (((0,), (0,)), ((), ())), preferred_element_type=jnp.float32
                )
                numer = part if numer is None else numer + part
            rows = slice(h * HEAD_SIZE, (h + 1) * HEAD_SIZE)
            if kind != 0:
                total = total + stat_ref[heads + h : heads + h + 1, q0 : q0 + TILE] * keep
                numer = numer + acc_ref[rows, q0 : q0 + TILE] * keep
            if last:
                done = numer / total
                halves[0].append(jnp.concatenate([done[0:32], done[64:96]], axis=0))
                halves[1].append(jnp.concatenate([done[32:64], done[96:128]], axis=0))
            else:
                acc_out[rows, q0 : q0 + TILE] = numer
                stat_out[h : h + 1, q0 : q0 + TILE] = top
                stat_out[heads + h : heads + h + 1, q0 : q0 + TILE] = total
        if last:
            for core in range(2):
                for p in range(0, heads, 2):
                    both = jnp.concatenate(halves[core][p : p + 2], axis=0).T.astype(jnp.bfloat16)
                    for to in range(core, out_ref.shape[0], 2):
                        out_ref[to, q0 : q0 + TILE, p * 64 : p * 64 + 128] = both


VMEM = pl.BlockSpec(memory_space=pltpu.VMEM)
SMEM = pl.BlockSpec(memory_space=pltpu.SMEM)


def attend(kind, last, heads, *args):
    width = heads * HEAD_SIZE
    if last:
        out = jax.ShapeDtypeStruct((8, TOK, width // 2), jnp.bfloat16)
    else:
        out = (
            jax.ShapeDtypeStruct((width, TOK), jnp.float32),
            jax.ShapeDtypeStruct((2 * heads, TOK), jnp.float32),
        )
    return pl.pallas_call(
        functools.partial(attend_kernel, kind, last, heads),
        out_shape=out,
        in_specs=[VMEM] * len(args),
        out_specs=VMEM if last else (VMEM, VMEM),
        compiler_params=pltpu.CompilerParams(vmem_limit_bytes=16 << 20),
        cost_estimate=pl.CostEstimate(
            flops=4 * TOK * TOK * width, bytes_accessed=2 * 1024 * 1024, transcendentals=TOK * TOK * heads
        ),
    )(*args)


def project_kernel(counts, cut, pos_ref, a_ref, *refs):
    w_refs, (own_ref, other_ref, a_full, w_full) = refs[:-4], refs[-4:]
    share = a_ref.shape[2]
    for t in range(a_ref.shape[0]):
        a_full[:, t * share : (t + 1) * share] = a_ref[t]
    k = 0
    for count, ref in zip(counts, w_refs):
        for i in range(count):
            place = pl.ds(pl.multiple_of(pos_ref[k] * 32, 32), 32)
            w_full[place, :] = ref[i * 32 : i * 32 + 32, :]
            k += 1
    main, own, width = cut
    other = width - own
    for n0 in range(0, width, 256):
        n1 = min(n0 + 256, width)
        got = jnp.dot(a_full[...], w_full[:, n0:n1], preferred_element_type=jnp.float32).T
        for lo, hi, ref, base in (
            (0, main, own_ref, 0),
            (main, main + other, other_ref, 0),
            (main + other, width, own_ref, main),
        ):
            s0, s1 = max(lo, n0), min(hi, n1)
            if s0 < s1:
                ref[base + s0 - lo : base + s1 - lo, :] = got[s0 - n0 : s1 - n0].astype(ref.dtype)


def project(counts, cut, pos, dealt, w_arrays):
    depth = sum(counts) * 32
    own, width = cut[1:]
    return pl.pallas_call(
        functools.partial(project_kernel, counts, cut),
        out_shape=(
            jax.ShapeDtypeStruct((own, TOK), jnp.float32),
            jax.ShapeDtypeStruct((width - own, TOK), jnp.bfloat16),
        ),
        in_specs=[SMEM] + [VMEM] * (1 + len(w_arrays)),
        out_specs=(VMEM, VMEM),
        scratch_shapes=[pltpu.VMEM((TOK, depth), jnp.bfloat16), pltpu.VMEM((depth, w_arrays[0].shape[1]), jnp.bfloat16)],
        name="project",
        compiler_params=pltpu.CompilerParams(vmem_limit_bytes=36 << 20),
        cost_estimate=pl.CostEstimate(
            flops=2 * TOK * depth * width, bytes_accessed=12 * 1024 * 1024, transcendentals=0
        ),
    )(pos, dealt, *w_arrays)


def along(value, axis, by):
    n = lax.axis_size(axis)
    return lax.ppermute(value, axis, [(i, (i + by) % n) for i in range(n)])


def moved(z, y, by, along_z):
    return ((z + by) % 8, y) if along_z else (z, (y + by) % 8)


def spot(z, y, core):
    return (z * 8 + y) * 2 + core


def spread(value):
    groups = []
    for core in range(2):
        for k in range(4):
            members = [(i, k + 4 * j) for i in range(8) for j in range(2)]
            groups.append([spot(a, b, core) if core == 0 else spot(b, a, core) for a, b in members])
    copies = jnp.broadcast_to(value[None], (16,) + value.shape)
    got = lax.all_to_all(copies, ("z", "y", "core"), 0, 0, axis_index_groups=groups)
    return got.reshape(16 * value.shape[0], value.shape[1])


def ring(value, by):
    pairs = []
    for z in range(8):
        for y in range(8):
            for core in range(2):
                pairs.append((spot(z, y, core), spot(*moved(z, y, by, core == 1), core)))
    return lax.ppermute(value, ("z", "y", "core"), pairs)


def layer(query_states, rotated_key_states, value_state_rows, doc_ids, w_out):
    heads = query_states.shape[1] // HEAD_SIZE
    zs, ys = lax.axis_size("z"), lax.axis_size("y")
    z, y, core = (lax.axis_index(n) for n in ("z", "y", "core"))
    blocks = zs * ys
    onward = [(i, i + 1) for i in range(blocks - 1)]
    block = z * ys + y

    docs_row = jnp.broadcast_to(doc_ids.astype(jnp.bfloat16)[None, :], (16, TOK))
    packed = jnp.concatenate(
        [jnp.concatenate([rotated_key_states, value_state_rows], axis=1), docs_row], axis=0
    )
    one_back = lax.ppermute(packed, ("z", "y"), onward)
    two_back = lax.ppermute(one_back, ("z", "y"), onward)

    part, cols = w_out.shape[0] // 2, w_out.shape[1]
    main = cols // 128 * 128
    keep_w = jnp.where(core == 0, w_out[:part], w_out[part:])
    send_w = jnp.where(core == 0, w_out[part:], w_out[:part])
    got_w = along(send_w, "core", 1)
    fill = -2 * cols % 128
    seed = jnp.concatenate(
        [keep_w[:, :main], got_w, keep_w[:, main:], jnp.zeros((part, fill), w_out.dtype)], axis=1
    )
    own_cut = (main, cols, 2 * cols)

    home = spread(seed)
    below, above = ring(home, 1), ring(home, -1)
    mid = home.shape[0] // 2
    whole = [home, below, above, ring(below[:mid], 1), ring(above[mid:], -1)]
    b = jnp.where(core == 0, y, z)
    block_a, block_b = [], []
    for off, lo, hi in ((0, 0, 16), (-1, 0, 16), (1, 0, 16), (2, 0, 8), (2, 8, 16)):
        i = jnp.arange(lo, hi, dtype=jnp.int32)
        block_a.append(i >> 1)
        block_b.append(((b + off) & 3) + 4 * (i & 1))
    block_a, block_b = jnp.concatenate(block_a), jnp.concatenate(block_b)
    wz = jnp.where(core == 0, block_a, block_b)
    wy = jnp.where(core == 0, block_b, block_a)
    pos = wz * 8 + wy

    row = doc_ids[None, :]
    col = jnp.broadcast_to(doc_ids[:, None], (TOK, 128))
    row_one = jnp.where(block >= 1, row, -1 - row)
    row_two = jnp.where(block >= 2, row, -1 - row)
    acc, stat = attend(0, False, heads, query_states, rotated_key_states, value_state_rows, row, col)
    acc, stat = attend(1, False, heads, query_states, one_back, row_one, acc, stat)
    mine = attend(2, True, heads, query_states, two_back, row_two, acc, stat)
    dealt = lax.all_to_all(mine, ("x", "core"), 0, 0)
    own, other = project((16, 16, 16, 8, 8), own_cut, pos.astype(jnp.int32), dealt, whole)
    back = along(other, "core", 1)
    return (own + back.astype(jnp.float32)).astype(jnp.bfloat16).T


def solution(mesh):
    zs, ys = 8, 8
    fine = Mesh(mesh.devices.reshape(zs, ys, 4, 2), ("z", "y", "x", "core"))
    ctx, tp = ("z", "y"), ("x", "core")
    return jax.shard_map(
        layer,
        mesh=fine,
        in_specs=(P(ctx, tp), P(ctx, tp), P(ctx, tp), P(ctx), P(ctx, tp)),
        out_specs=P(ctx, tp),
        check_vma=False,
    )
```

```python
import functools
import jax
import jax.numpy as jnp
from jax import lax
from jax.experimental import pallas as pl
from jax.experimental.pallas import tpu as pltpu
from jax.sharding import Mesh
from jax.sharding import PartitionSpec as P


HEAD_SIZE = 128
NEG = -1e30
EXP_SCALE = 168.0 ** (-0.5) * 1.4426950408889634
TOK = 512
TILE = 256


def visible_tile(kind, k0, q0, rows, cols):
    key = lax.broadcasted_iota(jnp.int32, (rows, cols), 0) + k0
    query = lax.broadcasted_iota(jnp.int32, (rows, cols), 1) + q0
    if kind == 0:
        return key <= query
    if kind == 2:
        return key > query
    return None


def tile_needed(kind, k0, q0):
    if kind == 0:
        return k0 <= q0 + TILE - 1
    if kind == 2:
        return k0 + TILE - 1 > q0
    return True


def attend_kernel(kind, last, heads, *refs):
    if kind == 0:
        q_ref, k_ref, v_ref, row_ref, col_ref, acc_out, stat_out = refs
        kv_ref = None
    elif last:
        q_ref, kv_ref, row_ref, acc_ref, stat_ref, out_ref = refs
    else:
        q_ref, kv_ref, row_ref, acc_ref, stat_ref, acc_out, stat_out = refs
    kv_heads = heads // 2
    half = kv_heads * HEAD_SIZE
    q_docs = row_ref[...]
    for q0 in range(0, TOK, TILE):
        tiles = [k0 for k0 in range(0, TOK, TILE) if tile_needed(kind, k0, q0)]
        allowed = []
        for k0 in tiles:
            grid = visible_tile(kind, k0, q0, TILE, TILE)
            if kind == 0:
                keys = col_ref[k0 : k0 + TILE, :]
                same = jnp.concatenate(
                    [keys == q_docs[:, q0 + c : q0 + c + 128] for c in range(0, TILE, 128)], axis=1
                )
            else:
                first = q_docs[:, 0:1]
                k_docs = kv_ref[TOK : TOK + 1, :].astype(jnp.float32).astype(jnp.int32)
                before = jnp.sum(jnp.where(k_docs == first, 0, 1), axis=1, keepdims=True)
                key = lax.broadcasted_iota(jnp.int32, (TILE, TILE), 0) + k0
                same = (key >= before) & (q_docs[:, q0 : q0 + TILE] == first)
            allowed.append(same if grid is None else same & grid)
        halves = ([], [])
        for h in range(heads):
            g = h // 2
            q = q_ref[q0 : q0 + TILE, h * HEAD_SIZE : (h + 1) * HEAD_SIZE]
            scores = []
            for k0, ok in zip(tiles, allowed):
                if kind == 0:
                    k = k_ref[k0 : k0 + TILE, g * HEAD_SIZE : (g + 1) * HEAD_SIZE]
                else:
                    k = kv_ref[k0 : k0 + TILE, g * HEAD_SIZE : (g + 1) * HEAD_SIZE]
                s = lax.dot_general(k, q, (((1,), (1,)), ((), ())), preferred_element_type=jnp.float32)
                scores.append(jnp.where(ok, s, NEG))
            top = functools.reduce(jnp.maximum, [jnp.max(s, axis=0, keepdims=True) for s in scores])
            if kind != 0:
                old_top = stat_ref[h : h + 1, q0 : q0 + TILE]
                top = jnp.maximum(top, old_top)
                keep = jnp.exp2((old_top - top) * EXP_SCALE)
            weights = [jnp.exp2((s - top) * EXP_SCALE) for s in scores]
            total = functools.reduce(jnp.add, [jnp.sum(w, axis=0, keepdims=True) for w in weights])
            numer = None
            for k0, w in zip(tiles, weights):
                if kind == 0:
                    v = v_ref[k0 : k0 + TILE, g * HEAD_SIZE : (g + 1) * HEAD_SIZE]
                else:
                    v = kv_ref[k0 : k0 + TILE, half + g * HEAD_SIZE : half + (g + 1) * HEAD_SIZE]
                part = lax.dot_general(
                    v, w.astype(jnp.bfloat16), (((0,), (0,)), ((), ())), preferred_element_type=jnp.float32
                )
                numer = part if numer is None else numer + part
            rows = slice(h * HEAD_SIZE, (h + 1) * HEAD_SIZE)
            if kind != 0:
                total = total + stat_ref[heads + h : heads + h + 1, q0 : q0 + TILE] * keep
                numer = numer + acc_ref[rows, q0 : q0 + TILE] * keep
            if last:
                done = numer / total
                halves[0].append(jnp.concatenate([done[0:32], done[64:96]], axis=0))
                halves[1].append(jnp.concatenate([done[32:64], done[96:128]], axis=0))
            else:
                acc_out[rows, q0 : q0 + TILE] = numer
                stat_out[h : h + 1, q0 : q0 + TILE] = top
                stat_out[heads + h : heads + h + 1, q0 : q0 + TILE] = total
        if last:
            for core in range(2):
                for p in range(0, heads, 2):
                    both = jnp.concatenate(halves[core][p : p + 2], axis=0).T.astype(jnp.bfloat16)
                    for to in range(core, out_ref.shape[0], 2):
                        out_ref[to, q0 : q0 + TILE, p * 64 : p * 64 + 128] = both


VMEM = pl.BlockSpec(memory_space=pltpu.VMEM)
SMEM = pl.BlockSpec(memory_space=pltpu.SMEM)


def attend(kind, last, heads, *args):
    width = heads * HEAD_SIZE
    if last:
        out = jax.ShapeDtypeStruct((8, TOK, width // 2), jnp.bfloat16)
    else:
        out = (
            jax.ShapeDtypeStruct((width, TOK), jnp.float32),
            jax.ShapeDtypeStruct((2 * heads, TOK), jnp.float32),
        )
    return pl.pallas_call(
        functools.partial(attend_kernel, kind, last, heads),
        out_shape=out,
        in_specs=[VMEM] * len(args),
        out_specs=VMEM if last else (VMEM, VMEM),
        compiler_params=pltpu.CompilerParams(vmem_limit_bytes=16 << 20),
        cost_estimate=pl.CostEstimate(
            flops=4 * TOK * TOK * width, bytes_accessed=2 * 1024 * 1024, transcendentals=TOK * TOK * heads
        ),
    )(*args)


def project_kernel(counts, pos_ref, a_ref, *refs):
    w_refs, (out_ref, a_full, w_full) = refs[:-3], refs[-3:]
    share = a_ref.shape[2]

    @pl.when(pl.program_id(0) == 0)
    def _():
        for t in range(a_ref.shape[0]):
            a_full[:, t * share : (t + 1) * share] = a_ref[t]

    k = 0
    for count, ref in zip(counts, w_refs):
        for i in range(count):
            place = pl.ds(pl.multiple_of(pos_ref[k] * 32, 32), 32)
            w_full[place, :] = ref[i * 32 : i * 32 + 32, :]
            k += 1
    got = jnp.dot(a_full[...], w_full[...], preferred_element_type=jnp.float32)
    out_ref[...] = got.T.astype(out_ref.dtype)


def project(counts, tile_of, kind, pos, dealt, w_arrays):
    depth = sum(counts) * 32
    return pl.pallas_call(
        functools.partial(project_kernel, counts),
        out_shape=jax.ShapeDtypeStruct((768, TOK), kind),
        grid=(3,),
        in_specs=[SMEM, pl.BlockSpec(dealt.shape, lambda i: (0, 0, 0), pipeline_mode=pl.Buffered(1))]
        + [pl.BlockSpec((w.shape[0], 256), lambda i: (0, tile_of(i))) for w in w_arrays],
        out_specs=pl.BlockSpec((256, TOK), lambda i: (i, 0)),
        scratch_shapes=[pltpu.VMEM((TOK, depth), jnp.bfloat16), pltpu.VMEM((depth, 256), jnp.bfloat16)],
        compiler_params=pltpu.CompilerParams(vmem_limit_bytes=20 << 20),
        cost_estimate=pl.CostEstimate(
            flops=2 * TOK * depth * 768, bytes_accessed=6 * 1024 * 1024, transcendentals=0
        ),
    )(pos, dealt, *w_arrays)


def along(value, axis, by):
    n = lax.axis_size(axis)
    return lax.ppermute(value, axis, [(i, (i + by) % n) for i in range(n)])


def moved(z, y, by, along_z):
    return ((z + by) % 8, y) if along_z else (z, (y + by) % 8)


def spot(z, y, core):
    return (z * 8 + y) * 2 + core


def spread(value):
    groups = []
    for core in range(2):
        for k in range(8):
            groups.append([spot(i, k, core) if core == 0 else spot(k, i, core) for i in range(8)])
    copies = jnp.broadcast_to(value[None], (8,) + value.shape)
    got = lax.all_to_all(copies, ("z", "y", "core"), 0, 0, axis_index_groups=groups)
    return got.reshape(8 * value.shape[0], value.shape[1])


def ring(value, by):
    pairs = []
    for z in range(8):
        for y in range(8):
            for core in range(2):
                pairs.append((spot(z, y, core), spot(*moved(z, y, by, core == 1), core)))
    return lax.ppermute(value, ("z", "y", "core"), pairs)


def layer(query_states, rotated_key_states, value_state_rows, doc_ids, w_out):
    heads = query_states.shape[1] // HEAD_SIZE
    zs, ys = lax.axis_size("z"), lax.axis_size("y")
    z, y, core = (lax.axis_index(n) for n in ("z", "y", "core"))
    blocks = zs * ys
    onward = [(i, i + 1) for i in range(blocks - 1)]
    block = z * ys + y

    docs_row = jnp.broadcast_to(doc_ids.astype(jnp.bfloat16)[None, :], (16, TOK))
    packed = jnp.concatenate(
        [jnp.concatenate([rotated_key_states, value_state_rows], axis=1), docs_row], axis=0
    )
    one_back = lax.ppermute(packed, ("z", "y"), onward)
    two_back = lax.ppermute(one_back, ("z", "y"), onward)

    part, cols = w_out.shape[0] // 2, w_out.shape[1]
    main = 512
    keep_w = jnp.where(core == 0, w_out[:part], w_out[part:])
    send_w = jnp.where(core == 0, w_out[part:], w_out[:part])
    got_w = along(send_w, "core", 1)
    fill = -2 * cols % 128
    seed = jnp.concatenate(
        [keep_w[:, :main], got_w, keep_w[:, main:], jnp.zeros((part, fill), w_out.dtype)], axis=1
    )

    whole = [spread(seed)]
    up = down = whole[0]
    offsets = [0]
    for step in range(1, 4):
        up, down = ring(up, 1), ring(down, -1)
        whole += [up, down]
        offsets += [-step, step]
    whole.append(ring(down, -1))
    offsets.append(4)
    spread_at = jnp.tile(jnp.arange(8, dtype=jnp.int32), 8)
    ring_at = jnp.repeat(jnp.array(offsets, jnp.int32), 8) + jnp.where(core == 0, y, z)
    wz = jnp.where(core == 0, spread_at, ring_at & 7)
    wy = jnp.where(core == 0, ring_at & 7, spread_at)
    pos = wz * 8 + wy

    row = doc_ids[None, :]
    col = jnp.broadcast_to(doc_ids[:, None], (TOK, 128))
    row_one = jnp.where(block >= 1, row, -1 - row)
    row_two = jnp.where(block >= 2, row, -1 - row)
    acc, stat = attend(0, False, heads, query_states, rotated_key_states, value_state_rows, row, col)
    acc, stat = attend(1, False, heads, query_states, one_back, row_one, acc, stat)
    mine = attend(2, True, heads, query_states, two_back, row_two, acc, stat)
    dealt = lax.all_to_all(mine, ("x", "core"), 0, 0)
    pos = pos.astype(jnp.int32)
    counts = (8,) * 8
    other = project(counts, lambda i: i + 2, jnp.bfloat16, pos, dealt, whole)
    back = along(other, "core", 1)
    own = project(counts, lambda i: jnp.where(i == 2, 5, i), jnp.float32, pos, dealt, whole)
    rest = own[main : main + 2 * cols - 1280]
    own = jnp.concatenate([own[:main], other[cols:].astype(jnp.float32), rest], axis=0)
    return (own + back[:cols].astype(jnp.float32)).astype(jnp.bfloat16).T


def solution(mesh):
    zs, ys = 8, 8
    fine = Mesh(mesh.devices.reshape(zs, ys, 4, 2), ("z", "y", "x", "core"))
    ctx, tp = ("z", "y"), ("x", "core")
    return jax.shard_map(
        layer,
        mesh=fine,
        in_specs=(P(ctx, tp), P(ctx, tp), P(ctx, tp), P(ctx), P(ctx, tp)),
        out_specs=P(ctx, tp),
        check_vma=False,
    )
```

```python
import functools
import jax
import jax.numpy as jnp
from jax import lax
from jax.experimental import pallas as pl
from jax.experimental.pallas import tpu as pltpu
from jax.sharding import Mesh
from jax.sharding import PartitionSpec as P


HEAD_SIZE = 128
NEG = -1e30
EXP_SCALE = 168.0 ** (-0.5) * 1.4426950408889634
TOK = 512
TILE = 256


def visible_tile(kind, k0, q0, rows, cols):
    key = lax.broadcasted_iota(jnp.int32, (rows, cols), 0) + k0
    query = lax.broadcasted_iota(jnp.int32, (rows, cols), 1) + q0
    if kind == 0:
        return key <= query
    if kind == 2:
        return key > query
    return None


def tile_needed(kind, k0, q0):
    if kind == 0:
        return k0 <= q0 + TILE - 1
    if kind == 2:
        return k0 + TILE - 1 > q0
    return True


def attend_kernel(kind, last, heads, *refs):
    if kind == 0:
        q_ref, k_ref, v_ref, row_ref, col_ref, acc_out, stat_out = refs
        kv_ref = None
    elif last:
        q_ref, kv_ref, row_ref, acc_ref, stat_ref, out_ref = refs
    else:
        q_ref, kv_ref, row_ref, acc_ref, stat_ref, acc_out, stat_out = refs
    kv_heads = heads // 2
    half = kv_heads * HEAD_SIZE
    q_docs = row_ref[...]
    for q0 in range(0, TOK, TILE):
        tiles = [k0 for k0 in range(0, TOK, TILE) if tile_needed(kind, k0, q0)]
        allowed = []
        for k0 in tiles:
            grid = visible_tile(kind, k0, q0, TILE, TILE)
            if kind == 0:
                keys = col_ref[k0 : k0 + TILE, :]
                same = jnp.concatenate(
                    [keys == q_docs[:, q0 + c : q0 + c + 128] for c in range(0, TILE, 128)], axis=1
                )
            else:
                first = q_docs[:, 0:1]
                k_docs = kv_ref[TOK : TOK + 1, :].astype(jnp.float32).astype(jnp.int32)
                before = jnp.sum(jnp.where(k_docs == first, 0, 1), axis=1, keepdims=True)
                key = lax.broadcasted_iota(jnp.int32, (TILE, TILE), 0) + k0
                same = (key >= before) & (q_docs[:, q0 : q0 + TILE] == first)
            allowed.append(same if grid is None else same & grid)
        halves = ([], [])
        for h in range(heads):
            g = h // 2
            q = q_ref[q0 : q0 + TILE, h * HEAD_SIZE : (h + 1) * HEAD_SIZE]
            scores = []
            for k0, ok in zip(tiles, allowed):
                if kind == 0:
                    k = k_ref[k0 : k0 + TILE, g * HEAD_SIZE : (g + 1) * HEAD_SIZE]
                else:
                    k = kv_ref[k0 : k0 + TILE, g * HEAD_SIZE : (g + 1) * HEAD_SIZE]
                s = lax.dot_general(k, q, (((1,), (1,)), ((), ())), preferred_element_type=jnp.float32)
                scores.append(jnp.where(ok, s, NEG))
            top = functools.reduce(jnp.maximum, [jnp.max(s, axis=0, keepdims=True) for s in scores])
            if kind != 0:
                old_top = stat_ref[h : h + 1, q0 : q0 + TILE]
                top = jnp.maximum(top, old_top)
                keep = jnp.exp2((old_top - top) * EXP_SCALE)
            weights = [jnp.exp2((s - top) * EXP_SCALE) for s in scores]
            total = functools.reduce(jnp.add, [jnp.sum(w, axis=0, keepdims=True) for w in weights])
            numer = None
            for k0, w in zip(tiles, weights):
                if kind == 0:
                    v = v_ref[k0 : k0 + TILE, g * HEAD_SIZE : (g + 1) * HEAD_SIZE]
                else:
                    v = kv_ref[k0 : k0 + TILE, half + g * HEAD_SIZE : half + (g + 1) * HEAD_SIZE]
                part = lax.dot_general(
                    v, w.astype(jnp.bfloat16), (((0,), (0,)), ((), ())), preferred_element_type=jnp.float32
                )
                numer = part if numer is None else numer + part
            rows = slice(h * HEAD_SIZE, (h + 1) * HEAD_SIZE)
            if kind != 0:
                total = total + stat_ref[heads + h : heads + h + 1, q0 : q0 + TILE] * keep
                numer = numer + acc_ref[rows, q0 : q0 + TILE] * keep
            if last:
                done = numer / total
                halves[0].append(jnp.concatenate([done[0:32], done[64:96]], axis=0))
                halves[1].append(jnp.concatenate([done[32:64], done[96:128]], axis=0))
            else:
                acc_out[rows, q0 : q0 + TILE] = numer
                stat_out[h : h + 1, q0 : q0 + TILE] = top
                stat_out[heads + h : heads + h + 1, q0 : q0 + TILE] = total
        if last:
            for core in range(2):
                for p in range(0, heads, 2):
                    both = jnp.concatenate(halves[core][p : p + 2], axis=0).T.astype(jnp.bfloat16)
                    for to in range(core, out_ref.shape[0], 2):
                        out_ref[to, q0 : q0 + TILE, p * 64 : p * 64 + 128] = both


VMEM = pl.BlockSpec(memory_space=pltpu.VMEM)
SMEM = pl.BlockSpec(memory_space=pltpu.SMEM)


def attend(kind, last, heads, *args):
    width = heads * HEAD_SIZE
    if last:
        out = jax.ShapeDtypeStruct((8, TOK, width // 2), jnp.bfloat16)
    else:
        out = (
            jax.ShapeDtypeStruct((width, TOK), jnp.float32),
            jax.ShapeDtypeStruct((2 * heads, TOK), jnp.float32),
        )
    return pl.pallas_call(
        functools.partial(attend_kernel, kind, last, heads),
        out_shape=out,
        in_specs=[VMEM] * len(args),
        out_specs=VMEM if last else (VMEM, VMEM),
        compiler_params=pltpu.CompilerParams(vmem_limit_bytes=16 << 20),
        cost_estimate=pl.CostEstimate(
            flops=4 * TOK * TOK * width, bytes_accessed=2 * 1024 * 1024, transcendentals=TOK * TOK * heads
        ),
    )(*args)


def begin_kernel(cuts, pos_ref, a_ref, *refs):
    w_refs, (own_ref, other_ref, sel_ref, a_full, a_turn, w_full) = refs[:-6], refs[-6:]
    share = a_ref.shape[2]
    for t in range(a_ref.shape[0]):
        a_full[:, t * share : (t + 1) * share] = a_ref[t]
        a_turn[t * share : (t + 1) * share, :] = a_ref[t].T
    k = 0
    for ref in w_refs:
        for i in range(8):
            w_full[pl.ds(pl.multiple_of(pos_ref[k] * 32, 32), 32), :] = ref[i * 32 : i * 32 + 32, :]
            k += 1
    for i in range(8):
        place = pl.ds(pl.multiple_of(pos_ref[k + i] * 32, 32), 32)
        w_full[place, :] = jnp.zeros((32, w_full.shape[1]), w_full.dtype)
        sel_ref[i * 32 : i * 32 + 32, :] = a_turn[place, :]
    main, split, width = cuts
    for n0 in range(0, width, 256):
        n1 = min(n0 + 256, width)
        got = jnp.dot(a_full[...], w_full[:, n0:n1], preferred_element_type=jnp.float32).T
        for lo, hi, ref, base in ((0, main, own_ref, 0), (main, split, other_ref, 0), (split, width, own_ref, main)):
            s0, s1 = max(lo, n0), min(hi, n1)
            if s0 < s1:
                ref[base + s0 - lo : base + s1 - lo, :] = got[s0 - n0 : s1 - n0]


def begin(cuts, pos, dealt, w_arrays):
    main, split, width = cuts
    depth = 64 * 32
    cols = w_arrays[0].shape[1]
    return pl.pallas_call(
        functools.partial(begin_kernel, cuts),
        out_shape=(
            jax.ShapeDtypeStruct((width - split + main, TOK), jnp.float32),
            jax.ShapeDtypeStruct((split - main, TOK), jnp.float32),
            jax.ShapeDtypeStruct((256, TOK), jnp.bfloat16),
        ),
        in_specs=[SMEM] + [VMEM] * (1 + len(w_arrays)),
        out_specs=(VMEM,) * 3,
        scratch_shapes=[
            pltpu.VMEM((TOK, depth), jnp.bfloat16),
            pltpu.VMEM((depth, TOK), jnp.bfloat16),
            pltpu.VMEM((depth, cols), jnp.bfloat16),
        ],
        name="begin",
        compiler_params=pltpu.CompilerParams(vmem_limit_bytes=30 << 20),
        cost_estimate=pl.CostEstimate(
            flops=2 * TOK * depth * width, bytes_accessed=12 * 1024 * 1024, transcendentals=0
        ),
    )(pos, dealt, *w_arrays)


def finish_kernel(pieces, acc_ref, sel_ref, w_ref, out_ref):
    for row, col, skip, size in pieces:
        got = lax.dot_general(
            w_ref[:, col : col + skip + size],
            sel_ref[...],
            (((0,), (0,)), ((), ())),
            preferred_element_type=jnp.float32,
        )
        total = acc_ref[row : row + size, :] + got[skip : skip + size]
        out_ref[row : row + size, :] = total.astype(out_ref.dtype)


def finish(pieces, kind, acc, sel, w):
    return pl.pallas_call(
        functools.partial(finish_kernel, pieces),
        out_shape=jax.ShapeDtypeStruct(acc.shape, kind),
        in_specs=[VMEM] * 3,
        out_specs=VMEM,
        compiler_params=pltpu.CompilerParams(vmem_limit_bytes=12 << 20),
        cost_estimate=pl.CostEstimate(
            flops=2 * TOK * 256 * acc.shape[0], bytes_accessed=3 * 1024 * 1024, transcendentals=0
        ),
    )(acc, sel, w)


def along(value, axis, by):
    n = lax.axis_size(axis)
    return lax.ppermute(value, axis, [(i, (i + by) % n) for i in range(n)])


def moved(z, y, by, along_z):
    return ((z + by) % 8, y) if along_z else (z, (y + by) % 8)


def spot(z, y, core):
    return (z * 8 + y) * 2 + core


def spread(value):
    groups = []
    for core in range(2):
        for k in range(8):
            groups.append([spot(i, k, core) if core == 0 else spot(k, i, core) for i in range(8)])
    copies = jnp.broadcast_to(value[None], (8,) + value.shape)
    got = lax.all_to_all(copies, ("z", "y", "core"), 0, 0, axis_index_groups=groups)
    return got.reshape(8 * value.shape[0], value.shape[1])


def ring(value, by):
    pairs = []
    for z in range(8):
        for y in range(8):
            for core in range(2):
                pairs.append((spot(z, y, core), spot(*moved(z, y, by, core == 1), core)))
    return lax.ppermute(value, ("z", "y", "core"), pairs)


def layer(query_states, rotated_key_states, value_state_rows, doc_ids, w_out):
    heads = query_states.shape[1] // HEAD_SIZE
    zs, ys = lax.axis_size("z"), lax.axis_size("y")
    z, y, core = (lax.axis_index(n) for n in ("z", "y", "core"))
    blocks = zs * ys
    onward = [(i, i + 1) for i in range(blocks - 1)]
    block = z * ys + y

    docs_row = jnp.broadcast_to(doc_ids.astype(jnp.bfloat16)[None, :], (16, TOK))
    packed = jnp.concatenate(
        [jnp.concatenate([rotated_key_states, value_state_rows], axis=1), docs_row], axis=0
    )
    one_back = lax.ppermute(packed, ("z", "y"), onward)
    two_back = lax.ppermute(one_back, ("z", "y"), onward)

    part, cols = w_out.shape[0] // 2, w_out.shape[1]
    main = 512
    keep_w = jnp.where(core == 0, w_out[:part], w_out[part:])
    send_w = jnp.where(core == 0, w_out[part:], w_out[:part])
    got_w = along(send_w, "core", 1)
    fill = -2 * cols % 128
    seed = jnp.concatenate(
        [keep_w[:, :main], got_w, keep_w[:, main:], jnp.zeros((part, fill), w_out.dtype)], axis=1
    )

    whole = [spread(seed)]
    up = down = whole[0]
    offsets = [0]
    for step in range(1, 4):
        up, down = ring(up, 1), ring(down, -1)
        whole += [up, down]
        offsets += [-step, step]
    whole.append(ring(down, -1))
    offsets.append(4)
    spread_at = jnp.tile(jnp.arange(8, dtype=jnp.int32), 8)
    ring_at = jnp.repeat(jnp.array(offsets, jnp.int32), 8) + jnp.where(core == 0, y, z)
    wz = jnp.where(core == 0, spread_at, ring_at & 7)
    wy = jnp.where(core == 0, ring_at & 7, spread_at)
    pos = wz * 8 + wy

    row = doc_ids[None, :]
    col = jnp.broadcast_to(doc_ids[:, None], (TOK, 128))
    row_one = jnp.where(block >= 1, row, -1 - row)
    row_two = jnp.where(block >= 2, row, -1 - row)
    acc, stat = attend(0, False, heads, query_states, rotated_key_states, value_state_rows, row, col)
    acc, stat = attend(1, False, heads, query_states, one_back, row_one, acc, stat)
    mine = attend(2, True, heads, query_states, two_back, row_two, acc, stat)
    dealt = lax.all_to_all(mine, ("x", "core"), 0, 0)
    pos = pos.astype(jnp.int32)
    split, width = main + cols, 2 * cols
    own, other, sel = begin((main, split, width), pos, dealt, whole[:-1])
    other = finish(((0, main, 0, cols),), jnp.bfloat16, other, sel, whole[-1])
    back = along(other, "core", 1)
    skip = split % 128
    own_pieces = ((0, 0, 0, main), (main, split - skip, skip, width - split))
    own = finish(own_pieces, jnp.float32, own, sel, whole[-1])
    return (own + back.astype(jnp.float32)).astype(jnp.bfloat16).T


def solution(mesh):
    zs, ys = 8, 8
    fine = Mesh(mesh.devices.reshape(zs, ys, 4, 2), ("z", "y", "x", "core"))
    ctx, tp = ("z", "y"), ("x", "core")
    return jax.shard_map(
        layer,
        mesh=fine,
        in_specs=(P(ctx, tp), P(ctx, tp), P(ctx, tp), P(ctx), P(ctx, tp)),
        out_specs=P(ctx, tp),
        check_vma=False,
    )
```

```python
import functools
import jax
import jax.numpy as jnp
from jax import lax
from jax.experimental import pallas as pl
from jax.experimental.pallas import tpu as pltpu
from jax.sharding import Mesh
from jax.sharding import PartitionSpec as P


HEAD_SIZE = 128
NEG = -1e30
EXP_SCALE = 168.0 ** (-0.5) * 1.4426950408889634
TOK = 512
TILE = 256


def visible_tile(kind, k0, q0, rows, cols):
    key = lax.broadcasted_iota(jnp.int32, (rows, cols), 0) + k0
    query = lax.broadcasted_iota(jnp.int32, (rows, cols), 1) + q0
    if kind == 0:
        return key <= query
    if kind == 2:
        return key > query
    return None


def tile_needed(kind, k0, q0):
    if kind == 0:
        return k0 <= q0 + TILE - 1
    if kind == 2:
        return k0 + TILE - 1 > q0
    return True


def attend_kernel(kind, last, heads, *refs):
    if kind == 0:
        q_ref, k_ref, v_ref, row_ref, col_ref, acc_out, stat_out = refs
        kv_ref = None
    elif last:
        q_ref, kv_ref, row_ref, acc_ref, stat_ref, out_ref = refs
    else:
        q_ref, kv_ref, row_ref, acc_ref, stat_ref, acc_out, stat_out = refs
    kv_heads = heads // 2
    half = kv_heads * HEAD_SIZE
    q_docs = row_ref[...]
    for q0 in range(0, TOK, TILE):
        tiles = [k0 for k0 in range(0, TOK, TILE) if tile_needed(kind, k0, q0)]
        allowed = []
        for k0 in tiles:
            grid = visible_tile(kind, k0, q0, TILE, TILE)
            if kind == 0:
                keys = col_ref[k0 : k0 + TILE, :]
                same = jnp.concatenate(
                    [keys == q_docs[:, q0 + c : q0 + c + 128] for c in range(0, TILE, 128)], axis=1
                )
            else:
                first = q_docs[:, 0:1]
                k_docs = kv_ref[TOK : TOK + 1, :].astype(jnp.float32).astype(jnp.int32)
                before = jnp.sum(jnp.where(k_docs == first, 0, 1), axis=1, keepdims=True)
                key = lax.broadcasted_iota(jnp.int32, (TILE, TILE), 0) + k0
                same = (key >= before) & (q_docs[:, q0 : q0 + TILE] == first)
            allowed.append(same if grid is None else same & grid)
        halves = ([], [])
        for h in range(heads):
            g = h // 2
            q = q_ref[q0 : q0 + TILE, h * HEAD_SIZE : (h + 1) * HEAD_SIZE]
            scores = []
            for k0, ok in zip(tiles, allowed):
                if kind == 0:
                    k = k_ref[k0 : k0 + TILE, g * HEAD_SIZE : (g + 1) * HEAD_SIZE]
                else:
                    k = kv_ref[k0 : k0 + TILE, g * HEAD_SIZE : (g + 1) * HEAD_SIZE]
                s = lax.dot_general(k, q, (((1,), (1,)), ((), ())), preferred_element_type=jnp.float32)
                scores.append(jnp.where(ok, s, NEG))
            top = functools.reduce(jnp.maximum, [jnp.max(s, axis=0, keepdims=True) for s in scores])
            if kind != 0:
                old_top = stat_ref[h : h + 1, q0 : q0 + TILE]
                top = jnp.maximum(top, old_top)
                keep = jnp.exp2((old_top - top) * EXP_SCALE)
            weights = [jnp.exp2((s - top) * EXP_SCALE) for s in scores]
            total = functools.reduce(jnp.add, [jnp.sum(w, axis=0, keepdims=True) for w in weights])
            numer = None
            for k0, w in zip(tiles, weights):
                if kind == 0:
                    v = v_ref[k0 : k0 + TILE, g * HEAD_SIZE : (g + 1) * HEAD_SIZE]
                else:
                    v = kv_ref[k0 : k0 + TILE, half + g * HEAD_SIZE : half + (g + 1) * HEAD_SIZE]
                part = lax.dot_general(
                    v, w.astype(jnp.bfloat16), (((0,), (0,)), ((), ())), preferred_element_type=jnp.float32
                )
                numer = part if numer is None else numer + part
            rows = slice(h * HEAD_SIZE, (h + 1) * HEAD_SIZE)
            if kind != 0:
                total = total + stat_ref[heads + h : heads + h + 1, q0 : q0 + TILE] * keep
                numer = numer + acc_ref[rows, q0 : q0 + TILE] * keep
            if last:
                done = numer / total
                halves[0].append(jnp.concatenate([done[0:32], done[64:96]], axis=0))
                halves[1].append(jnp.concatenate([done[32:64], done[96:128]], axis=0))
            else:
                acc_out[rows, q0 : q0 + TILE] = numer
                stat_out[h : h + 1, q0 : q0 + TILE] = top
                stat_out[heads + h : heads + h + 1, q0 : q0 + TILE] = total
        if last:
            for core in range(2):
                for p in range(0, heads, 2):
                    both = jnp.concatenate(halves[core][p : p + 2], axis=0).T.astype(jnp.bfloat16)
                    for to in range(core, out_ref.shape[0], 2):
                        out_ref[to, q0 : q0 + TILE, p * 64 : p * 64 + 128] = both


VMEM = pl.BlockSpec(memory_space=pltpu.VMEM)
SMEM = pl.BlockSpec(memory_space=pltpu.SMEM)


def attend(kind, last, heads, *args):
    width = heads * HEAD_SIZE
    if last:
        out = jax.ShapeDtypeStruct((8, TOK, width // 2), jnp.bfloat16)
    else:
        out = (
            jax.ShapeDtypeStruct((width, TOK), jnp.float32),
            jax.ShapeDtypeStruct((2 * heads, TOK), jnp.float32),
        )
    return pl.pallas_call(
        functools.partial(attend_kernel, kind, last, heads),
        out_shape=out,
        in_specs=[VMEM] * len(args),
        out_specs=VMEM if last else (VMEM, VMEM),
        compiler_params=pltpu.CompilerParams(vmem_limit_bytes=16 << 20),
        cost_estimate=pl.CostEstimate(
            flops=4 * TOK * TOK * width, bytes_accessed=2 * 1024 * 1024, transcendentals=TOK * TOK * heads
        ),
    )(*args)


def begin_kernel(name, ranges, *refs):
    refs = list(refs)
    pos_ref, a_ref = refs.pop(0), refs.pop(0)
    sum_ref = refs.pop(0) if name == "more" else None
    w_refs, (acc_ref, sel_ref, a_full, a_turn, w_full) = refs[:-5], refs[-5:]
    share = a_ref.shape[2]
    for t in range(a_ref.shape[0]):
        a_full[:, t * share : (t + 1) * share] = a_ref[t]
        a_turn[t * share : (t + 1) * share, :] = a_ref[t].T
    for lo, hi, row, skip in ranges:
        k = 0
        for ref in w_refs:
            for i in range(8):
                place = pl.ds(pl.multiple_of(pos_ref[k] * 32, 32), 32)
                w_full[place, 0 : hi - lo] = ref[i * 32 : i * 32 + 32, lo:hi]
                k += 1
        for i in range(8):
            place = pl.ds(pl.multiple_of(pos_ref[k + i] * 32, 32), 32)
            w_full[place, 0 : hi - lo] = jnp.zeros((32, hi - lo), w_full.dtype)
        got = jnp.dot(a_full[...], w_full[:, 0 : hi - lo], preferred_element_type=jnp.float32).T
        size = hi - lo - skip
        got = got[skip:]
        if sum_ref is not None:
            got = got + sum_ref[row : row + size, :]
        acc_ref[row : row + size, :] = got
    for i in range(8):
        place = pl.ds(pl.multiple_of(pos_ref[56 + i] * 32, 32), 32)
        sel_ref[i * 32 : i * 32 + 32, :] = a_turn[place, :]


def begin(name, ranges, cols, pos, dealt, sums, w_arrays):
    depth = 64 * 32
    args = [pos, dealt] + ([sums] if name == "more" else []) + list(w_arrays)
    return pl.pallas_call(
        functools.partial(begin_kernel, name, ranges),
        out_shape=(
            jax.ShapeDtypeStruct((cols, TOK), jnp.float32),
            jax.ShapeDtypeStruct((256, TOK), jnp.bfloat16),
        ),
        in_specs=[SMEM] + [VMEM] * (len(args) - 1),
        out_specs=(VMEM,) * 2,
        scratch_shapes=[
            pltpu.VMEM((TOK, depth), jnp.bfloat16),
            pltpu.VMEM((depth, TOK), jnp.bfloat16),
            pltpu.VMEM((depth, 256), jnp.bfloat16),
        ],
        compiler_params=pltpu.CompilerParams(vmem_limit_bytes=24 << 20),
        cost_estimate=pl.CostEstimate(
            flops=2 * TOK * depth * cols, bytes_accessed=8 * 1024 * 1024, transcendentals=0
        ),
    )(*args)


def finish_kernel(main, split, acc_ref, kept_ref, given_ref, w_ref, out_ref):
    cols = acc_ref.shape[0]
    turned = lambda lo, hi, ref: lax.dot_general(
        w_ref[:, lo:hi], ref[...], (((0,), (0,)), ((), ())), preferred_element_type=jnp.float32
    )
    skip = split % 128
    kept = jnp.concatenate(
        [turned(0, main, kept_ref), turned(split - skip, 2 * cols, kept_ref)[skip:]], axis=0
    )
    out_ref[...] = (acc_ref[...] + kept + turned(main, split, given_ref)).astype(out_ref.dtype)


def finish(main, split, acc, kept, given, w):
    return pl.pallas_call(
        functools.partial(finish_kernel, main, split),
        out_shape=jax.ShapeDtypeStruct(acc.shape, jnp.bfloat16),
        in_specs=[VMEM] * 4,
        out_specs=VMEM,
        name="finish",
        compiler_params=pltpu.CompilerParams(vmem_limit_bytes=16 << 20),
        cost_estimate=pl.CostEstimate(
            flops=4 * TOK * 256 * acc.shape[0], bytes_accessed=3 * 1024 * 1024, transcendentals=0
        ),
    )(acc, kept, given, w)


def along(value, axis, by):
    n = lax.axis_size(axis)
    return lax.ppermute(value, axis, [(i, (i + by) % n) for i in range(n)])


def moved(z, y, by, along_z):
    return ((z + by) % 8, y) if along_z else (z, (y + by) % 8)


def spot(z, y, core):
    return (z * 8 + y) * 2 + core


def spread(value):
    groups = []
    for core in range(2):
        for k in range(8):
            groups.append([spot(i, k, core) if core == 0 else spot(k, i, core) for i in range(8)])
    copies = jnp.broadcast_to(value[None], (8,) + value.shape)
    got = lax.all_to_all(copies, ("z", "y", "core"), 0, 0, axis_index_groups=groups)
    return got.reshape(8 * value.shape[0], value.shape[1])


def ring(value, by):
    pairs = []
    for z in range(8):
        for y in range(8):
            for core in range(2):
                pairs.append((spot(z, y, core), spot(*moved(z, y, by, core == 1), core)))
    return lax.ppermute(value, ("z", "y", "core"), pairs)


def layer(query_states, rotated_key_states, value_state_rows, doc_ids, w_out):
    heads = query_states.shape[1] // HEAD_SIZE
    zs, ys = lax.axis_size("z"), lax.axis_size("y")
    z, y, core = (lax.axis_index(n) for n in ("z", "y", "core"))
    blocks = zs * ys
    onward = [(i, i + 1) for i in range(blocks - 1)]
    block = z * ys + y

    docs_row = jnp.broadcast_to(doc_ids.astype(jnp.bfloat16)[None, :], (16, TOK))
    packed = jnp.concatenate(
        [jnp.concatenate([rotated_key_states, value_state_rows], axis=1), docs_row], axis=0
    )
    one_back = lax.ppermute(packed, ("z", "y"), onward)
    two_back = lax.ppermute(one_back, ("z", "y"), onward)

    part, cols = w_out.shape[0] // 2, w_out.shape[1]
    main = 512
    keep_w = jnp.where(core == 0, w_out[:part], w_out[part:])
    rest_w = jnp.where(core == 0, w_out[part:], w_out[:part])
    fill = -2 * cols % 128
    seed = jnp.concatenate(
        [keep_w[:, :main], rest_w, keep_w[:, main:], jnp.zeros((part, fill), w_out.dtype)], axis=1
    )

    whole = [spread(seed)]
    up = down = whole[0]
    offsets = [0]
    for step in range(1, 4):
        up, down = ring(up, 1), ring(down, -1)
        whole += [up, down]
        offsets += [-step, step]
    whole.append(ring(down, -1))
    offsets.append(4)
    spread_at = jnp.tile(jnp.arange(8, dtype=jnp.int32), 8)
    ring_at = jnp.repeat(jnp.array(offsets, jnp.int32), 8) + jnp.where(core == 0, y, z)
    wz = jnp.where(core == 0, spread_at, ring_at & 7)
    wy = jnp.where(core == 0, ring_at & 7, spread_at)
    pos = wz * 8 + wy

    row = doc_ids[None, :]
    col = jnp.broadcast_to(doc_ids[:, None], (TOK, 128))
    row_one = jnp.where(block >= 1, row, -1 - row)
    row_two = jnp.where(block >= 2, row, -1 - row)
    acc, stat = attend(0, False, heads, query_states, rotated_key_states, value_state_rows, row, col)
    acc, stat = attend(1, False, heads, query_states, one_back, row_one, acc, stat)
    mine = attend(2, True, heads, query_states, two_back, row_two, acc, stat)
    dealt = lax.all_to_all(mine, ("x", "core"), 0, 0)
    pos = pos.astype(jnp.int32)
    given = along(dealt, "core", 1)
    split = main + cols
    skip = split % 128
    kept_ranges = ((0, 256, 0, 0), (256, main, 256, 0), (split - skip, 2 * cols, main, skip))
    rest_ranges = tuple((c, min(c + 256, split), c - main, 0) for c in range(main, split, 256))
    acc, kept = begin("begin", kept_ranges, cols, pos, dealt, None, whole[:-1])
    acc, other = begin("more", rest_ranges, cols, pos, given, acc, whole[:-1])
    return finish(main, split, acc, kept, other, whole[-1]).T


def solution(mesh):
    zs, ys = 8, 8
    fine = Mesh(mesh.devices.reshape(zs, ys, 4, 2), ("z", "y", "x", "core"))
    ctx, tp = ("z", "y"), ("x", "core")
    return jax.shard_map(
        layer,
        mesh=fine,
        in_specs=(P(ctx, tp), P(ctx, tp), P(ctx, tp), P(ctx), P(ctx, tp)),
        out_specs=P(ctx, tp),
        check_vma=False,
    )
```

```python
import functools
import jax
import jax.numpy as jnp
from jax import lax
from jax.experimental import pallas as pl
from jax.experimental.pallas import tpu as pltpu
from jax.sharding import Mesh
from jax.sharding import PartitionSpec as P


HEAD_SIZE = 128
NEG = -1e30
EXP_SCALE = 168.0 ** (-0.5) * 1.4426950408889634
TOK = 512
TILE = 256


def visible_tile(kind, k0, q0, rows, cols):
    key = lax.broadcasted_iota(jnp.int32, (rows, cols), 0) + k0
    query = lax.broadcasted_iota(jnp.int32, (rows, cols), 1) + q0
    if kind == 0:
        return key <= query
    if kind == 2:
        return key > query
    return None


def tile_needed(kind, k0, q0):
    if kind == 0:
        return k0 <= q0 + TILE - 1
    if kind == 2:
        return k0 + TILE - 1 > q0
    return True


def attend_kernel(kind, last, heads, *refs):
    if kind == 0:
        q_ref, k_ref, v_ref, row_ref, col_ref, acc_out, stat_out = refs
        kv_ref = None
    elif last:
        at_ref, q_ref, kv_ref, row_ref, acc_ref, stat_ref, out_ref = refs
    else:
        at_ref, q_ref, kv_ref, row_ref, acc_ref, stat_ref, acc_out, stat_out = refs
    kv_heads = heads // 2
    half = kv_heads * HEAD_SIZE
    q_docs = row_ref[...]
    for q0 in range(0, TOK, TILE):
        tiles = [k0 for k0 in range(0, TOK, TILE) if tile_needed(kind, k0, q0)]
        allowed = []
        for k0 in tiles:
            grid = visible_tile(kind, k0, q0, TILE, TILE)
            if kind == 0:
                keys = col_ref[k0 : k0 + TILE, :]
                same = jnp.concatenate(
                    [keys == q_docs[:, q0 + c : q0 + c + 128] for c in range(0, TILE, 128)], axis=1
                )
            else:
                first = q_docs[:, 0:1]
                k_docs = kv_ref[TOK : TOK + 1, :].astype(jnp.float32).astype(jnp.int32)
                before = jnp.sum(jnp.where(k_docs == first, 0, 1), axis=1, keepdims=True)
                before = jnp.where(at_ref[0] >= kind, before, TOK)
                key = lax.broadcasted_iota(jnp.int32, (TILE, TILE), 0) + k0
                same = (key >= before) & (q_docs[:, q0 : q0 + TILE] == first)
            allowed.append(same if grid is None else same & grid)
        halves = ([], [])
        for h in range(heads):
            g = h // 2
            q = q_ref[q0 : q0 + TILE, h * HEAD_SIZE : (h + 1) * HEAD_SIZE]
            scores = []
            for k0, ok in zip(tiles, allowed):
                if kind == 0:
                    k = k_ref[k0 : k0 + TILE, g * HEAD_SIZE : (g + 1) * HEAD_SIZE]
                else:
                    k = kv_ref[k0 : k0 + TILE, g * HEAD_SIZE : (g + 1) * HEAD_SIZE]
                s = lax.dot_general(k, q, (((1,), (1,)), ((), ())), preferred_element_type=jnp.float32)
                scores.append(jnp.where(ok, s, NEG))
            top = functools.reduce(jnp.maximum, [jnp.max(s, axis=0, keepdims=True) for s in scores])
            if kind != 0:
                old_top = stat_ref[h : h + 1, q0 : q0 + TILE]
                top = jnp.maximum(top, old_top)
                keep = jnp.exp2((old_top - top) * EXP_SCALE)
            weights = [jnp.exp2((s - top) * EXP_SCALE) for s in scores]
            total = functools.reduce(jnp.add, [jnp.sum(w, axis=0, keepdims=True) for w in weights])
            numer = None
            for k0, w in zip(tiles, weights):
                if kind == 0:
                    v = v_ref[k0 : k0 + TILE, g * HEAD_SIZE : (g + 1) * HEAD_SIZE]
                else:
                    v = kv_ref[k0 : k0 + TILE, half + g * HEAD_SIZE : half + (g + 1) * HEAD_SIZE]
                part = lax.dot_general(
                    v, w.astype(jnp.bfloat16), (((0,), (0,)), ((), ())), preferred_element_type=jnp.float32
                )
                numer = part if numer is None else numer + part
            rows = slice(h * HEAD_SIZE, (h + 1) * HEAD_SIZE)
            if kind != 0:
                total = total + stat_ref[heads + h : heads + h + 1, q0 : q0 + TILE] * keep
                numer = numer + acc_ref[rows, q0 : q0 + TILE] * keep
            if last:
                done = numer / total
                halves[0].append(jnp.concatenate([done[0:32], done[64:96]], axis=0))
                halves[1].append(jnp.concatenate([done[32:64], done[96:128]], axis=0))
            else:
                acc_out[rows, q0 : q0 + TILE] = numer
                stat_out[h : h + 1, q0 : q0 + TILE] = top
                stat_out[heads + h : heads + h + 1, q0 : q0 + TILE] = total
        if last:
            for core in range(2):
                for p in range(0, heads, 2):
                    both = jnp.concatenate(halves[core][p : p + 2], axis=0).T.astype(jnp.bfloat16)
                    for to in range(core, out_ref.shape[0], 2):
                        out_ref[to, q0 : q0 + TILE, p * 64 : p * 64 + 128] = both


VMEM = pl.BlockSpec(memory_space=pltpu.VMEM)
SMEM = pl.BlockSpec(memory_space=pltpu.SMEM)


def attend(kind, last, heads, *args):
    width = heads * HEAD_SIZE
    if last:
        out = jax.ShapeDtypeStruct((8, TOK, width // 2), jnp.bfloat16)
    else:
        out = (
            jax.ShapeDtypeStruct((width, TOK), jnp.float32),
            jax.ShapeDtypeStruct((2 * heads, TOK), jnp.float32),
        )
    return pl.pallas_call(
        functools.partial(attend_kernel, kind, last, heads),
        out_shape=out,
        in_specs=([SMEM] if kind else []) + [VMEM] * (len(args) - (1 if kind else 0)),
        out_specs=VMEM if last else (VMEM, VMEM),
        compiler_params=pltpu.CompilerParams(vmem_limit_bytes=16 << 20),
        cost_estimate=pl.CostEstimate(
            flops=4 * TOK * TOK * width, bytes_accessed=2 * 1024 * 1024, transcendentals=TOK * TOK * heads
        ),
    )(*args)


def prepare_kernel(main, at_ref, k_ref, v_ref, row_ref, w_ref, kv_ref, copies_ref):
    width = k_ref.shape[1]
    kv_ref[0:TOK, 0:width] = k_ref[...]
    kv_ref[0:TOK, width:] = v_ref[...]
    kv_ref[TOK:, :] = jnp.broadcast_to(row_ref[...].astype(jnp.float32), (16, TOK)).astype(jnp.bfloat16)
    part, cols = w_ref.shape[0] // 2, w_ref.shape[1]
    low, high = w_ref[:part, :].astype(jnp.float32), w_ref[part:, :].astype(jnp.float32)
    first_core = at_ref[1] == 0
    keep, rest = jnp.where(first_core, low, high), jnp.where(first_core, high, low)
    fill = jnp.zeros((part, -2 * cols % 128), jnp.float32)
    seed = jnp.concatenate([keep[:, :main], rest, keep[:, main:], fill], axis=1).astype(jnp.bfloat16)
    for to in range(copies_ref.shape[0]):
        copies_ref[to] = seed


def prepare(main, at, k, v, row, w):
    part, cols = w.shape[0] // 2, w.shape[1]
    return pl.pallas_call(
        functools.partial(prepare_kernel, main),
        out_shape=(
            jax.ShapeDtypeStruct((TOK + 16, 2 * k.shape[1]), jnp.bfloat16),
            jax.ShapeDtypeStruct((8, part, 2 * cols + -2 * cols % 128), jnp.bfloat16),
        ),
        in_specs=[SMEM] + [VMEM] * 4,
        out_specs=(VMEM, VMEM),
        name="prepare",
        compiler_params=pltpu.CompilerParams(vmem_limit_bytes=60 << 20),
        cost_estimate=pl.CostEstimate(flops=0, bytes_accessed=2 * 1024 * 1024, transcendentals=0),
    )(at, k, v, row, w)


def begin_kernel(name, ranges, *refs):
    refs = list(refs)
    pos_ref, a_ref = refs.pop(0), refs.pop(0)
    sum_ref = refs.pop(0) if name == "more" else None
    w_refs, (acc_ref, sel_ref, a_full, a_turn, w_full) = refs[:-5], refs[-5:]
    share = a_ref.shape[2]
    for t in range(a_ref.shape[0]):
        a_full[:, t * share : (t + 1) * share] = a_ref[t]
        a_turn[t * share : (t + 1) * share, :] = a_ref[t].T
    for lo, hi, row, skip in ranges:
        k = 0
        for ref in w_refs:
            for i in range(8):
                place = pl.ds(pl.multiple_of(pos_ref[k] * 32, 32), 32)
                w_full[place, 0 : hi - lo] = ref[i * 32 : i * 32 + 32, lo:hi]
                k += 1
        for i in range(8):
            place = pl.ds(pl.multiple_of(pos_ref[k + i] * 32, 32), 32)
            w_full[place, 0 : hi - lo] = jnp.zeros((32, hi - lo), w_full.dtype)
        got = jnp.dot(a_full[...], w_full[:, 0 : hi - lo], preferred_element_type=jnp.float32).T
        size = hi - lo - skip
        got = got[skip:]
        if sum_ref is not None:
            got = got + sum_ref[row : row + size, :]
        acc_ref[row : row + size, :] = got
    for i in range(8):
        place = pl.ds(pl.multiple_of(pos_ref[56 + i] * 32, 32), 32)
        sel_ref[i * 32 : i * 32 + 32, :] = a_turn[place, :]


def begin(name, ranges, cols, pos, dealt, sums, w_arrays):
    depth = 64 * 32
    args = [pos, dealt] + ([sums] if name == "more" else []) + list(w_arrays)
    return pl.pallas_call(
        functools.partial(begin_kernel, name, ranges),
        out_shape=(
            jax.ShapeDtypeStruct((cols, TOK), jnp.float32),
            jax.ShapeDtypeStruct((256, TOK), jnp.bfloat16),
        ),
        in_specs=[SMEM] + [VMEM] * (len(args) - 1),
        out_specs=(VMEM,) * 2,
        scratch_shapes=[
            pltpu.VMEM((TOK, depth), jnp.bfloat16),
            pltpu.VMEM((depth, TOK), jnp.bfloat16),
            pltpu.VMEM((depth, 256), jnp.bfloat16),
        ],
        compiler_params=pltpu.CompilerParams(vmem_limit_bytes=24 << 20),
        cost_estimate=pl.CostEstimate(
            flops=2 * TOK * depth * cols, bytes_accessed=8 * 1024 * 1024, transcendentals=0
        ),
    )(*args)


def finish_kernel(main, split, acc_ref, kept_ref, given_ref, w_ref, out_ref):
    cols = acc_ref.shape[0]
    turned = lambda lo, hi, ref: lax.dot_general(
        w_ref[:, lo:hi], ref[...], (((0,), (0,)), ((), ())), preferred_element_type=jnp.float32
    )
    skip = split % 128
    kept = jnp.concatenate(
        [turned(0, main, kept_ref), turned(split - skip, 2 * cols, kept_ref)[skip:]], axis=0
    )
    out_ref[...] = (acc_ref[...] + kept + turned(main, split, given_ref)).astype(out_ref.dtype)


def finish(main, split, acc, kept, given, w):
    return pl.pallas_call(
        functools.partial(finish_kernel, main, split),
        out_shape=jax.ShapeDtypeStruct(acc.shape, jnp.bfloat16),
        in_specs=[VMEM] * 4,
        out_specs=VMEM,
        name="finish",
        compiler_params=pltpu.CompilerParams(vmem_limit_bytes=16 << 20),
        cost_estimate=pl.CostEstimate(
            flops=4 * TOK * 256 * acc.shape[0], bytes_accessed=3 * 1024 * 1024, transcendentals=0
        ),
    )(acc, kept, given, w)


def along(value, axis, by):
    n = lax.axis_size(axis)
    return lax.ppermute(value, axis, [(i, (i + by) % n) for i in range(n)])


def moved(z, y, by, along_z):
    return ((z + by) % 8, y) if along_z else (z, (y + by) % 8)


def spot(z, y, core):
    return (z * 8 + y) * 2 + core


def spread(copies):
    groups = []
    for core in range(2):
        for k in range(8):
            groups.append([spot(i, k, core) if core == 0 else spot(k, i, core) for i in range(8)])
    got = lax.all_to_all(copies, ("z", "y", "core"), 0, 0, axis_index_groups=groups)
    return got.reshape(8 * copies.shape[1], copies.shape[2])


def ring(value, by):
    pairs = []
    for z in range(8):
        for y in range(8):
            for core in range(2):
                pairs.append((spot(z, y, core), spot(*moved(z, y, by, core == 1), core)))
    return lax.ppermute(value, ("z", "y", "core"), pairs)


def layer(query_states, rotated_key_states, value_state_rows, doc_ids, w_out):
    heads = query_states.shape[1] // HEAD_SIZE
    zs, ys = lax.axis_size("z"), lax.axis_size("y")
    z, y, core = (lax.axis_index(n) for n in ("z", "y", "core"))
    blocks = zs * ys
    onward = [(i, i + 1) for i in range(blocks - 1)]
    block = z * ys + y

    cols, main = w_out.shape[1], 512
    row = doc_ids[None, :]
    at = jnp.stack([block, core]).astype(jnp.int32)
    packed, copies = prepare(main, at, rotated_key_states, value_state_rows, row, w_out)
    one_back = lax.ppermute(packed, ("z", "y"), onward)
    two_back = lax.ppermute(one_back, ("z", "y"), onward)

    whole = [spread(copies)]
    up = down = whole[0]
    offsets = [0]
    for step in range(1, 4):
        up, down = ring(up, 1), ring(down, -1)
        whole += [up, down]
        offsets += [-step, step]
    whole.append(ring(down, -1))
    offsets.append(4)
    spread_at = jnp.tile(jnp.arange(8, dtype=jnp.int32), 8)
    ring_at = jnp.repeat(jnp.array(offsets, jnp.int32), 8) + jnp.where(core == 0, y, z)
    wz = jnp.where(core == 0, spread_at, ring_at & 7)
    wy = jnp.where(core == 0, ring_at & 7, spread_at)
    pos = wz * 8 + wy

    col = jnp.broadcast_to(doc_ids[:, None], (TOK, 128))
    acc, stat = attend(0, False, heads, query_states, rotated_key_states, value_state_rows, row, col)
    acc, stat = attend(1, False, heads, at, query_states, one_back, row, acc, stat)
    mine = attend(2, True, heads, at, query_states, two_back, row, acc, stat)
    dealt = lax.all_to_all(mine, ("x", "core"), 0, 0)
    pos = pos.astype(jnp.int32)
    given = along(dealt, "core", 1)
    split = main + cols
    skip = split % 128
    kept_ranges = ((0, 256, 0, 0), (256, main, 256, 0), (split - skip, 2 * cols, main, skip))
    rest_ranges = tuple((c, min(c + 256, split), c - main, 0) for c in range(main, split, 256))
    acc, kept = begin("begin", kept_ranges, cols, pos, dealt, None, whole[:-1])
    acc, other = begin("more", rest_ranges, cols, pos, given, acc, whole[:-1])
    return finish(main, split, acc, kept, other, whole[-1]).T


def solution(mesh):
    zs, ys = 8, 8
    fine = Mesh(mesh.devices.reshape(zs, ys, 4, 2), ("z", "y", "x", "core"))
    ctx, tp = ("z", "y"), ("x", "core")
    return jax.shard_map(
        layer,
        mesh=fine,
        in_specs=(P(ctx, tp), P(ctx, tp), P(ctx, tp), P(ctx), P(ctx, tp)),
        out_specs=P(ctx, tp),
        check_vma=False,
    )
```
